32 devices in a mesh: gx: 4 (over z), gy: 4 (over x, core), gz: 2 (over y).
Axes of the slice: x: 2, y: 2, z: 4, core: 2. Of those that a mesh axis runs over, the one named last changes fastest.
Arguments:
- element_ops: float32 [64, 64, 4096], P(None, None, ('gx', 'gy', 'gz')), may hold values from -0.5 to 48, as said below
- load_terms: float32 [64, 4096], P(None, ('gx', 'gy', 'gz')), may hold values from -16 to 16
- trial_velocity: float32 [3, 512, 4096], P(None, None, ('gx', 'gy', 'gz')), may hold values from -16 to 16
- tracer_coords: float32 [3, 65536], P(None, ('gx', 'gy', 'gz')), may hold values from -1 to 1
- tracer_old_velocity: float32 [3, 65536], P(None, ('gx', 'gy', 'gz')), may hold values from -6 to 6
- host_line: int32 [65536, 1], P(('gx', 'gy', 'gz')), may hold values from 0 to 3; in each aligned block of 2048 rows (0 to 2047, 2048 to 4095, ...) at most 1024 rows name the same one
- host_element_index: int32 [65536], P(('gx', 'gy', 'gz')), may hold values from 0 to 127
Outputs:
- pressure_fix: float32 [64, 4096], P(None, ('gx', 'gy', 'gz'))
- velocity: bfloat16 [3, 512, 4096], P(None, None, ('gx', 'gy', 'gz'))
- residual_power: float32 [], replicated
- tracer_velocity: float32 [3, 65536], P(None, ('gx', 'gy', 'gz'))
- new_coords: float32 [3, 65536], P(None, ('gx', 'gy', 'gz'))
The draws below stay inside these ranges and needn't reach their ends.
Inputs may be any that keep to these rules, and one draw needn't show every extreme that they name: `element_ops`: symmetric in its first two dimensions; every diagonal entry exceeds the sum of the magnitudes of the other entries of its row. `host_line`: among the 2048 tracers of one device, no host position is named more than 1024 times, a bound that some block reaches in every draw.
All inputs are finite; a program needn't handle non-finite values. Where the reference program divides by a largest or mean magnitude, that divisor is 1e-20 or more.
Results may differ from the reference program's by a relative error of at most 0.0029.
Values may be sent and summed in bfloat16 or wider, within the bound.
A program may use at most 64 MiB of HBM per device.

```python
import math
import jax
import jax.numpy as jnp
import numpy as np
from jax import lax

EX = 4
EY = 4
EZ = 8
E_DEV = 128
ELEMS = 4096
ELEMENTS_ALONG_Z = 16
SWEEPS = 4
TRACERS_DEVICE = 2048
CAP = 1024
TRACERS = 65536
N_GX = 4
N_GY = 4
N_GZ = 2


def height_scale(top_layer):
    element_index = jnp.arange(ELEMS, dtype=jnp.int32)
    device = element_index // E_DEV
    layer_index = device % N_GZ * EZ + element_index % E_DEV % EZ
    return 1.0 + (top_layer - 1.0) * layer_index.astype(jnp.float32) / max(ELEMENTS_ALONG_Z - 1, 1)


def draw_element_ops(key, part):
    keys = jax.random.split(jax.random.fold_in(key, 11), 3)
    top_layer = 10.0
    scale = jnp.exp(jax.random.uniform(keys[0], (ELEMS,), jnp.float32, 0.0, jnp.log(top_layer)))
    raw = jax.random.uniform(keys[1], (64, 64, ELEMS), jnp.float32, -1.0, 1.0)
    eye = jnp.eye(64, dtype=jnp.float32)[:, :, None]
    off = 0.5 * (raw + raw.transpose(1, 0, 2)) * (scale / 32.0)[None, None, :] * (1.0 - eye)
    mass = jax.random.uniform(keys[2], (64, ELEMS), jnp.float32, 0.2, 1.0) * scale[None, :]
    diagonal = jnp.sum(jnp.abs(off), axis=1) + mass
    return off + eye * diagonal[:, None, :]


def draw_load_terms(key, part):
    base = jax.random.fold_in(key, 23)
    rough = jnp.clip(jax.random.normal(base, (64, ELEMS), jnp.float32), -4.0, 4.0)
    return rough * height_scale(3.0)[None, :]


def draw_trial_velocity(key, part):
    base = jax.random.fold_in(key, 37)
    rough = jnp.clip(jax.random.normal(base, (3, 512, ELEMS), jnp.float32), -4.0, 4.0)
    return rough * height_scale(3.0)[None, None, :]


def plant(values, rng, smallest, top_value):
    dims = values.shape
    index_at = [jax.random.randint(jax.random.fold_in(rng, axis), (), 0, dims[axis]) for axis in range(len(dims))]
    values = values.at[tuple(index_at)].set(smallest)
    longest = dims.index(max(dims))
    index_at[longest] = (index_at[longest] + 1) % dims[longest]
    return values.at[tuple(index_at)].set(top_value)


def block_levels(key, extent, cuts, low, largest):
    loudness = 1.0
    for axis_at, blocks in cuts:
        heights = jax.random.uniform(jax.random.fold_in(jax.random.fold_in(key, 6), axis_at), (blocks,), jnp.float32, low / len(cuts), largest / len(cuts))
        loudness = loudness * jnp.repeat(jnp.exp(heights), extent[axis_at] // blocks).reshape((-1,) + (1,) * (len(extent) - 1 - axis_at))
    return loudness


def assign_block(stream_key, own, number, rows, count, top, reach, skew):
    ranking = jax.random.permutation(stream_key, count)
    crowded, usual = shares(count, rows * top, reach, skew, True), shares(count, rows * top, reach, skew, False)
    places = jnp.arange(count)

    def named(tallies, offset_by):
        used = int((tallies > 0).sum())
        fixed = max(1, used // 4)
        moved = fixed + (places - fixed + offset_by * (used - fixed)) % max(1, count - fixed)
        return jnp.zeros((count,), jnp.int32).at[ranking[jnp.where(places < fixed, places, moved)]].set(jnp.asarray(tallies, jnp.int32))

    tallies = jnp.where(number % 4 == 0, named(crowded, number // 4), named(usual, number - number // 4 - 1))
    mixed = jax.random.permutation(jax.random.fold_in(own, 3), count)
    source_of, sink = mixed[0:count // 2 * 2:2], mixed[1:count // 2 * 2:2]
    margin = jnp.minimum(tallies[source_of] - 1, reach - tallies[sink]) // 2
    margin = jnp.where((source_of == ranking[0]) | (sink == ranking[0]) | (tallies[sink] == 0), 0, jnp.maximum(margin, 0))
    moved = jax.random.randint(jax.random.fold_in(own, 4), (count // 2,), 0, 1 << 20) % (margin + 1)
    tallies = tallies.at[source_of].add(-moved).at[sink].add(moved)
    members = jnp.searchsorted(jnp.cumsum(tallies), jnp.arange(rows * top), side="right").astype(jnp.int32)
    table = members.reshape(top, rows).T
    table = table[jax.random.permutation(jax.random.fold_in(own, 1), rows)]
    offset_by = jax.random.randint(jax.random.fold_in(own, 2), (rows, 1), 0, top)
    return jnp.take_along_axis(table, (jnp.arange(top)[None, :] + offset_by) % top, axis=1)


def shares(number_of, total, reach, skew, full):
    weights = [(1 << 20) // math.isqrt(grade ** skew) + 1 for grade in range(1, number_of + 1)]
    largest = reach if full else min(reach, max(-(-total // number_of), total * weights[0] // sum(weights)))
    least = 1 if total - largest >= number_of - 1 else 0
    given, surplus = [largest] + [least] * (number_of - 1), total - largest - least * (number_of - 1)
    while surplus > 0:
        candidates = [i for i in range(1, number_of) if given[i] < largest] or [i for i in range(1, number_of) if given[i] < reach]
        pool, left = sum([weights[i] for i in candidates]), surplus
        for i in candidates:
            addition = min(reach - given[i], max(1, left * weights[i] // pool), surplus)
            given[i] = given[i] + addition
            surplus = surplus - addition
    return np.array(given)


def gaussian(rng, extent, width, bound, cuts=(), held_as=jnp.bfloat16):
    array = jax.random.normal(rng, extent, jnp.float32) * width
    if len(cuts) > 0:
        array = block_levels(rng, extent, cuts, -0.22, 0.18) * array
    return jnp.clip(array, min=-bound, max=bound).astype(held_as)


def setup_inputs(seed: int = 0) -> dict:
    key_list = jax.random.split(jax.random.key(seed), 8)
    element_ops = draw_element_ops(jax.random.fold_in(key_list[7], 71), 0)
    load_terms = draw_load_terms(jax.random.fold_in(key_list[7], 71), 0)
    trial_velocity = draw_trial_velocity(jax.random.fold_in(key_list[7], 71), 0)
    tracer_coords = jnp.clip(jax.random.uniform(key_list[3], (3, TRACERS), jnp.float32, -1.0, 1.0) * block_levels(key_list[3], (3, TRACERS), ((1, 32),), -0.4, 0.0), -1.0, 1.0)
    tracer_old_velocity = gaussian(key_list[4], (3, TRACERS), 1.0, 6.0, ((1, 32),), jnp.float32)
    host_line_keys = jax.random.split(jax.random.fold_in(key_list[5], 1), TRACERS // TRACERS_DEVICE)
    host_line_turns = jax.random.permutation(jax.random.fold_in(key_list[5], 3), TRACERS // TRACERS_DEVICE)
    host_line = jax.vmap(lambda own, number: assign_block(jax.random.fold_in(key_list[5], 2), own, number, TRACERS_DEVICE, N_GX, 1, CAP, 2))(host_line_keys, host_line_turns).reshape((TRACERS, 1))
    host_element_index = plant(jax.random.randint(key_list[6], (TRACERS,), 0, E_DEV), jax.random.fold_in(key_list[6], 1), 0, E_DEV - 1).astype(jnp.int32)
    return dict(element_ops=element_ops, load_terms=load_terms, trial_velocity=trial_velocity, tracer_coords=tracer_coords, tracer_old_velocity=tracer_old_velocity, host_line=host_line, host_element_index=host_element_index)


lower_bound = 0.25
upper_bound = 2.0
courant = 0.5
highest = lax.Precision.HIGHEST


def node_tables():
    coarse = -np.cos(np.pi * np.arange(4) / 3.0)
    fine = -np.cos(np.pi * np.arange(8) / 7.0)
    plain = np.zeros((8, 4))
    slope = np.zeros((8, 4))
    for target in range(8):
        for source in range(4):
            others = [other for other in range(4) if other != source]
            value = 1.0
            for other in others:
                value *= (fine[target] - coarse[other]) / (coarse[source] - coarse[other])
            plain[target, source] = value
            total = 0.0
            for skipped in others:
                term = 1.0 / (coarse[source] - coarse[skipped])
                for other in others:
                    if other != skipped:
                        term *= (fine[target] - coarse[other]) / (coarse[source] - coarse[other])
                total += term
            slope[target, source] = total
    return jnp.asarray(plain, jnp.float32), jnp.asarray(slope, jnp.float32), fine


def placement_matrix(count):
    node = jnp.arange(4)[:, None, None]
    element_index = jnp.arange(count)[None, :, None]
    point = jnp.arange(3 * count + 1)[None, None, :]
    return (point == 3 * element_index + node).astype(jnp.float32)


def to_grid(local, counts):
    stack = local.shape[0]
    cube = local.reshape(stack, 4, 4, 4, counts[0], counts[1], counts[2])
    step_x = jnp.einsum('sabcxyz,axg->sgbcyz', cube, placement_matrix(counts[0]), precision=highest)
    step_y = jnp.einsum('sgbcyz,byh->sghcz', step_x, placement_matrix(counts[1]), precision=highest)
    return jnp.einsum('sghcz,czk->sghk', step_y, placement_matrix(counts[2]), precision=highest)


def from_grid(grid, counts):
    stack = grid.shape[0]
    step_z = jnp.einsum('sghk,czk->sghcz', grid, placement_matrix(counts[2]), precision=highest)
    step_y = jnp.einsum('sghcz,byh->sgbcyz', step_z, placement_matrix(counts[1]), precision=highest)
    step_x = jnp.einsum('sgbcyz,axg->sabcxyz', step_y, placement_matrix(counts[0]), precision=highest)
    return step_x.reshape(stack, 64, -1)


def smooth(operators, loads, assemble):
    diagonal = jnp.diagonal(operators, axis1=0, axis2=1).T
    right, weight = assemble((loads, diagonal))
    center = 0.5 * (upper_bound + lower_bound)
    radius = 0.5 * (upper_bound - lower_bound)
    sigma = center / radius
    rho = 1.0 / sigma
    solution = jnp.zeros_like(right)
    residual = right
    apply_update = residual / (center * weight)
    for sweep in range(SWEEPS):
        solution = solution + apply_update
        image = assemble((jnp.einsum('ije,je->ie', operators, apply_update, precision=highest),))[0]
        residual = residual - image
        if sweep + 1 < SWEEPS:
            rho_next = 1.0 / (2.0 * sigma - rho)
            apply_update = rho_next * rho * apply_update + (2.0 * rho_next / radius) * residual / weight
            rho = rho_next
    return solution, residual


def corrected_velocity(pressure, trial, plain, slope):
    count = pressure.shape[1]
    field = pressure.reshape(4, 4, 4, count)
    z_plain = jnp.einsum('mc,abce->abme', plain, field, precision=highest)
    z_slope = jnp.einsum('mc,abce->abme', slope, field, precision=highest)
    y_plain = jnp.einsum('lb,abme->alme', plain, z_plain, precision=highest)
    y_slope = jnp.einsum('lb,abme->alme', slope, z_plain, precision=highest)
    y_zslope = jnp.einsum('lb,abme->alme', plain, z_slope, precision=highest)
    grad_x = jnp.einsum('ka,alme->klme', slope, y_plain, precision=highest)
    grad_y = jnp.einsum('ka,alme->klme', plain, y_slope, precision=highest)
    grad_z = jnp.einsum('ka,alme->klme', plain, y_zslope, precision=highest)
    gradient = jnp.stack([grad_x, grad_y, grad_z]).reshape(3, 512, count)
    return (trial - gradient).astype(jnp.bfloat16)


def lagrange_weights(points, fine):
    rows = []
    for target in range(8):
        value = jnp.ones_like(points)
        for other in range(8):
            if other != target:
                value = value * ((points - float(fine[other])) / float(fine[target] - fine[other]))
        rows.append(value)
    return jnp.stack(rows)


def interpolate(field, element_index, points, fine, block):
    count = element_index.shape[0]
    size = math.gcd(count, block)
    groups = count // size

    def one_group(pieces):
        index, where = pieces
        rows = jnp.take(field, index, axis=2).reshape(3, 8, 8, 8, size)
        w_x = lagrange_weights(where[0], fine)
        w_y = lagrange_weights(where[1], fine)
        w_z = lagrange_weights(where[2], fine)
        inner = jnp.sum(rows * w_z[None, None, None], axis=3)
        inner = jnp.sum(inner * w_y[None, None], axis=2)
        return jnp.sum(inner * w_x[None], axis=1)

    grouped = points.reshape(3, groups, size).transpose(1, 0, 2)
    result = lax.map(one_group, (element_index.reshape(groups, size), grouped))
    return result.transpose(1, 0, 2).reshape(3, count)


def advance_tracers(field, element_index, payload, stride, fine, block):
    flows = interpolate(field, element_index, payload[:3], fine, block)
    moved = payload[:3] + stride * (1.5 * flows - 0.5 * payload[3:])
    return jnp.concatenate([moved, flows], axis=0)


def reference(element_ops, load_terms, trial_velocity, tracer_coords, tracer_old_velocity, host_line, host_element_index):
    plain, slope, fine = node_tables()
    counts = (EX * N_GX, EY * N_GY, EZ * N_GZ)

    def assemble(parts):
        local = jnp.stack(parts)
        stack = local.shape[0]
        ordered = local.reshape(stack, 64, N_GX, N_GY, N_GZ, EX, EY, EZ)
        ordered = ordered.transpose(0, 1, 2, 5, 3, 6, 4, 7).reshape(stack, 64, -1)
        summed = from_grid(to_grid(ordered, counts), counts)
        summed = summed.reshape(stack, 64, N_GX, EX, N_GY, EY, N_GZ, EZ)
        summed = summed.transpose(0, 1, 2, 4, 6, 3, 5, 7).reshape(stack, 64, -1)
        return tuple(summed[index] for index in range(stack))

    solution, residual = smooth(element_ops, load_terms, assemble)
    velocity = corrected_velocity(solution, trial_velocity, plain, slope)
    speed = jnp.max(jnp.sum(jnp.abs(velocity.astype(jnp.float32)), axis=0))
    power = jnp.sum(residual * residual) / (64.0 * ELEMS)
    stride = courant / (speed + 1e-6)
    device = jnp.arange(TRACERS, dtype=jnp.int32) // TRACERS_DEVICE
    row_y = (device // N_GZ) % N_GY
    row_z = device % N_GZ
    owner = (host_line[:, 0] * N_GY + row_y) * N_GZ + row_z
    column = (owner * E_DEV + host_element_index).astype(jnp.int32)
    payload = jnp.concatenate([tracer_coords, tracer_old_velocity], axis=0)
    moved = advance_tracers(velocity, column, payload, stride, fine, 8192)
    return solution, velocity, power, moved[3:], moved[:3]
```

```python
import functools

import jax
import jax.numpy as jnp
import numpy as np
from jax import lax
from jax.experimental import pallas as pl
from jax.experimental.pallas import tpu as pltpu
from jax.sharding import PartitionSpec as P

EX = 4
EY = 4
EZ = 8
SWEEPS = 4
NODES = 64
FACE = 16
LANES = 128
FINE = 512

lower_bound = 0.25
upper_bound = 2.0
courant = 0.5
AXES = ("gx", "gy", "gz")
COUNTS = (EX, EY, EZ)
STEPS = (EY * EZ, EZ, 1)
MESH = pl.DeviceIdType.MESH
FINISH = 4
BRICK_VMEM = 24 * 1024 * 1024
OUT_VMEM = 4 * 1024 * 1024


def node_tables():
    coarse = -np.cos(np.pi * np.arange(4) / 3.0)
    fine = -np.cos(np.pi * np.arange(8) / 7.0)
    plain = np.zeros((8, 4))
    slope = np.zeros((8, 4))
    for target in range(8):
        for source in range(4):
            others = [other for other in range(4) if other != source]
            value = 1.0
            for other in others:
                value *= (fine[target] - coarse[other]) / (coarse[source] - coarse[other])
            plain[target, source] = value
            total = 0.0
            for skipped in others:
                term = 1.0 / (coarse[source] - coarse[skipped])
                for other in others:
                    if other != skipped:
                        term *= (fine[target] - coarse[other]) / (coarse[source] - coarse[other])
                total += term
            slope[target, source] = total
    return plain, slope, fine


def gradient_matrix():
    plain, slope, _ = node_tables()
    rows = [
        np.kron(np.kron(slope, plain), plain),
        np.kron(np.kron(plain, slope), plain),
        np.kron(np.kron(plain, plain), slope),
    ]
    full = np.concatenate(rows, axis=0).astype(np.float32)
    high = full.astype(jnp.bfloat16)
    low = (full - high.astype(np.float32)).astype(jnp.bfloat16)
    return np.concatenate([high, high, low, high], axis=1)


def weight_table():
    fine = node_tables()[2]
    table = np.zeros((8, 8, LANES), np.float32)
    for target in range(8):
        others = [other for other in range(8) if other != target]
        scale = 1.0
        for j, other in enumerate(others):
            table[j, target] = fine[other]
            scale /= fine[target] - fine[other]
        table[7, target] = scale
    return table


DIRS = [
    (i, j, k)
    for size in (3, 2, 1)
    for i in (-1, 0, 1)
    for j in (-1, 0, 1)
    for k in (-1, 0, 1)
    if abs(i) + abs(j) + abs(k) == size
]


def slot_of(way):
    return (way[0] + 1) * 9 + (way[1] + 1) * 3 + way[2] + 1


def face_rows(way):
    x, y, z = (None if w == 0 else (3 if w > 0 else 0) for w in way)
    if x is not None and y is not None and z is not None:
        return [(16 * x + 4 * y + z, 1, 1)]
    if x is not None and y is not None:
        return [(16 * x + 4 * y, 4, 1)]
    if x is not None and z is not None:
        return [(16 * x + z, 4, 4)]
    if y is not None and z is not None:
        return [(4 * y + z, 4, 16)]
    if x is not None:
        return [(16 * x, 16, 1)]
    if y is not None:
        return [(16 * a + 4 * y, 4, 1) for a in range(4)]
    return [(z, 16, 4)]


def length_of(way):
    return sum(size for _, size, _ in face_rows(way))


def rows_of(piece):
    start, size, stride = piece
    return (pl.ds(start, size, stride=stride) if stride > 1 else pl.ds(start, size), slice(None))


def bit_moves(size):
    return [1 << bit for bit in range(size.bit_length()) if 1 << bit < size]


def kernel(
    sizes,
    direct,
    ops_hbm,
    load_hbm,
    trial_hbm,
    grad_hbm,
    table_hbm,
    coords_hbm,
    old_hbm,
    line_hbm,
    index_hbm,
    sol_ref,
    vel,
    power_ref,
    flow_ref,
    moved_ref,
    ops,
    load,
    trial,
    grad,
    table_ref,
    coords,
    old,
    host,
    index,
    pay_ref,
    old_ref,
    upd,
    res,
    wgt,
    img,
    work,
    wide,
    face_out,
    face_in,
    pay_in,
    back_out,
    back_in,
    red_out,
    red_in,
    local_sem,
    face_send,
    face_recv,
    pay_send,
    pay_recv,
    back_send,
    back_recv,
    red_send,
    red_recv,
):
    me = [lax.axis_index(axis) for axis in AXES]
    line = sizes[0]
    groups = pay_ref.shape[1]

    def edge(d, step):
        return me[d] < sizes[d] - 1 if step > 0 else me[d] > 0

    def exists(way):
        tests = [edge(d, way[d]) for d in range(3) if way[d] != 0]
        return functools.reduce(jnp.logical_and, tests)

    present = {way: exists(way) for way in DIRS}

    def beside(way):
        return {AXES[d]: me[d] + way[d] for d in range(3) if way[d] != 0}

    def along(offset):
        there = me[0]
        for bit in bit_moves(line):
            if offset & bit:
                there = there + bit * (1 - 2 * lax.rem(me[0] // bit, 2))
        return {AXES[0]: there}

    def shifted(offset):
        return {
            AXES[d]: lax.rem(me[d] + offset[d], sizes[d]) for d in range(3) if offset[d] != 0
        }

    spans = [range(size) for size in sizes]
    if direct:
        teams = [[(i, j, k) for i in spans[0] for j in spans[1] for k in spans[2]]]
        seats = [(me[0] * sizes[1] + me[1]) * sizes[2] + me[2]]
    else:
        teams = [[(0, j, k) for j in spans[1] for k in spans[2]], [(i, 0, 0) for i in spans[0]]]
        seats = [me[1] * sizes[2] + me[2], me[0]]
    bases = [sum(len(team) for team in teams[:t]) for t in range(len(teams))]

    barrier = pltpu.get_barrier_semaphore()
    for way in DIRS:

        @pl.when(present[way])
        def _():
            pl.semaphore_signal(barrier, inc=1, device_id=beside(way), device_id_type=MESH)

    partners = [along(offset) for offset in range(1, line)]
    if not direct:
        partners += [shifted(offset) for team in teams for offset in team[1:]]
    for partner in partners:
        pl.semaphore_signal(barrier, inc=1, device_id=partner, device_id_type=MESH)

    pairs = [
        (ops_hbm, ops),
        (load_hbm, load),
        (line_hbm, host),
        (index_hbm, index),
        (coords_hbm, coords),
        (old_hbm, old),
        (table_hbm, table_ref),
        (trial_hbm, trial),
        (grad_hbm, grad),
    ]
    loads = [
        pltpu.make_async_copy(src, dst, local_sem.at[i]) for i, (src, dst) in enumerate(pairs)
    ]
    for i in (1, 0, 2, 3, 4, 5, 6, 7, 8):
        loads[i].start()

    for way in DIRS:

        @pl.when(jnp.logical_not(present[way]))
        def _():
            for x in range(SWEEPS + 1):
                face_in[x, slot_of(way)] = jnp.zeros((2 * FACE, LANES), jnp.float32)

    lane = lax.broadcasted_iota(jnp.int32, (40, LANES), 1)
    place = [lane // (EY * EZ), lane // EZ % EY, lane % EZ]

    def parts_of(x):
        return 2 if x == 0 else 1

    def face_copy(x, way):
        rows = parts_of(x) * length_of(way)
        there = slot_of(tuple(-w for w in way))
        return pltpu.make_async_remote_copy(
            src_ref=face_out.at[x, slot_of(way), pl.ds(0, rows)],
            dst_ref=face_in.at[x, there, pl.ds(0, rows)],
            send_sem=face_send.at[x, slot_of(way)],
            recv_sem=face_recv.at[x, there],
            device_id=beside(way),
            device_id_type=MESH,
        )

    def fill_faces(x, parts, ways):
        for way in ways:
            at = 0
            for ref in parts:
                for piece in face_rows(way):
                    face_out[x, slot_of(way), at : at + piece[1]] = ref[rows_of(piece)]
                    at += piece[1]

    def start_faces(x, ways):
        for way in ways:

            @pl.when(present[way])
            def _():
                face_copy(x, way).start()

    def drain_faces(x):
        for way in DIRS:

            @pl.when(present[way])
            def _():
                face_copy(x, way).wait_send()

    def open_faces(x, parts):
        for group in (DIRS[:8], DIRS[8:20], DIRS[20:]):
            fill_faces(x, parts, group)
            start_faces(x, group)

    def combine(d, pieces):
        at = 0
        for size, *places in pieces:
            for s, (ref, piece) in enumerate(places):
                work[s, at : at + size] = ref[rows_of(piece)]
            at += size
        count, step = COUNTS[d], STEPS[d]
        far = (count - 1) * step
        total = -(-at // 8) * 8
        low, high, before, after = (work[s, 0:total] for s in range(4))
        where_at = place[d][0:total]
        new = (
            low
            + jnp.where(
                where_at > 0,
                pltpu.roll(high, step, 1),
                pltpu.roll(before, (LANES - far) % LANES, 1),
            ),
            high
            + jnp.where(
                where_at < count - 1,
                pltpu.roll(low, LANES - step, 1),
                pltpu.roll(after, far, 1),
            ),
        )
        at = 0
        for size, *places in pieces:
            for s in range(2):
                ref, piece = places[s]
                ref[rows_of(piece)] = new[s][at : at + size]
            at += size

    def close_faces(x, parts):
        for way in DIRS:

            @pl.when(present[way])
            def _():
                face_copy(x, tuple(-w for w in way)).wait_recv()

        ends = (-1, 1)
        for p, ref in enumerate(parts):

            def got(way, start=0, size=None, stride=1):
                full = length_of(way)
                return (
                    face_in.at[x, slot_of(way)],
                    (p * full + start, full if size is None else size, stride),
                )

            pieces = [(16, (ref, (0, 16, 1)), (ref, (48, 16, 1)), got((-1, 0, 0)), got((1, 0, 0)))]
            for o in ends:
                for way in ((0, o, 0), (0, 0, o)):
                    lo, hi = (-1, *way[1:]), (1, *way[1:])
                    pieces.append((4, got(way, 0, 4), got(way, 12, 4), got(lo), got(hi)))
            for oy in ends:
                for oz in ends:
                    way = (0, oy, oz)
                    pieces.append(
                        (1, got(way, 0, 1), got(way, 3, 1), got((-1, oy, oz)), got((1, oy, oz)))
                    )
            combine(0, pieces)
            pieces = []
            for a in range(4):
                pieces.append(
                    (
                        4,
                        (ref, (16 * a, 4, 1)),
                        (ref, (16 * a + 12, 4, 1)),
                        got((0, -1, 0), 4 * a, 4),
                        got((0, 1, 0), 4 * a, 4),
                    )
                )
            for oz in ends:
                way = (0, 0, oz)
                pieces.append(
                    (4, got(way, 0, 4, 4), got(way, 3, 4, 4), got((0, -1, oz)), got((0, 1, oz)))
                )
            combine(1, pieces)
            combine(
                2,
                [(16, (ref, (0, 16, 4)), (ref, (3, 16, 4)), got((0, 0, -1)), got((0, 0, 1)))],
            )

    def apply_operator():
        def block(i, total):
            rows = upd[pl.ds(pl.multiple_of(8 * i, 8), 8), :]
            for j in range(8):
                total = total + ops[8 * i + j] * rows[j : j + 1, :]
            return total

        img[...] = lax.fori_loop(0, NODES // 8, block, jnp.zeros((NODES, LANES), jnp.float32))

    def pay_copy(offset):
        return pltpu.make_async_remote_copy(
            src_ref=pay_ref,
            dst_ref=pay_in.at[offset - 1],
            send_sem=pay_send.at[offset - 1],
            recv_sem=pay_recv.at[offset - 1],
            device_id=along(offset),
            device_id_type=MESH,
        )

    def back_copy(offset):
        return pltpu.make_async_remote_copy(
            src_ref=back_out.at[offset],
            dst_ref=back_in.at[offset - 1],
            send_sem=back_send.at[offset - 1],
            recv_sem=back_recv.at[offset - 1],
            device_id=along(offset),
            device_id_type=MESH,
        )

    def red_copy(kind, t, offset):
        return pltpu.make_async_remote_copy(
            src_ref=red_out.at[kind, t, pl.ds(0, 1)],
            dst_ref=red_in.at[kind, bases[t] + seats[t], pl.ds(0, 1)],
            send_sem=red_send.at[kind, bases[t] + offset],
            recv_sem=red_recv.at[kind, bases[t] + offset],
            device_id=shifted(teams[t][offset]),
            device_id_type=MESH,
        )

    def open_sums(kind, t, value):
        red_out[kind, t, 0:1] = value
        for offset in range(len(teams[t]) - 1, 0, -1):
            red_copy(kind, t, offset).start()
        red_in[kind, bases[t] + seats[t], 0:1] = value

    def close_sums(kind, t):
        for offset in range(1, len(teams[t])):
            red_copy(kind, t, offset).wait_recv()
        values = [red_in[kind, bases[t] + i, 0:1] for i in range(len(teams[t]))]
        join = jnp.add if kind else jnp.maximum
        while len(values) > 1:
            values = [
                join(*values[i : i + 2]) if i + 1 < len(values) else values[i]
                for i in range(0, len(values), 2)
            ]
        return values[0]

    def drain_sums(kind):
        for t, team in enumerate(teams):
            for offset in range(1, len(team)):
                red_copy(kind, t, offset).wait_send()

    loads[1].wait()
    loads[0].wait()
    res[...] = load[...]
    for n in range(NODES):
        wgt[n : n + 1, :] = ops[n, n : n + 1, :]
    fill_faces(0, (res, wgt), DIRS)
    for copy in loads[2:7]:
        copy.wait()
    pay_ref[3] = (host[...] * LANES + index[...]).astype(jnp.float32)
    for d in range(3):
        for g in range(groups):
            lanes = slice(g * LANES, (g + 1) * LANES)
            pay_ref[d, g : g + 1, :] = coords[d : d + 1, lanes]
            old_ref[d, g : g + 1, :] = old[d : d + 1, lanes]

    near = [sum(edge(d, step).astype(jnp.int32) for step in (-1, 1)) for d in range(3)]
    pl.semaphore_wait(
        barrier, len(partners) + (1 + near[0]) * (1 + near[1]) * (1 + near[2]) - 1
    )

    start_faces(0, DIRS)
    order = range(line - 1, 0, -1)
    for offset in order:
        pay_copy(offset).start()
    close_faces(0, (res, wgt))

    center = 0.5 * (upper_bound + lower_bound)
    radius = 0.5 * (upper_bound - lower_bound)
    sigma = center / radius
    rho = 1.0 / sigma
    upd[...] = res[...] / (center * wgt[...])
    sol_ref[...] = upd[...]
    for sweep in range(SWEEPS - 1):
        apply_operator()
        open_faces(sweep + 1, (img,))
        drain_faces(sweep)
        if sweep + 2 == SWEEPS:
            for copy in loads[7:]:
                copy.wait()
            for offset in order:
                pay_copy(offset).wait_send()
        close_faces(sweep + 1, (img,))
        left = res[...] - img[...]
        res[...] = left
        rho_next = 1.0 / (2.0 * sigma - rho)
        new = (rho_next * rho) * upd[...] + (2.0 * rho_next / radius) * left / wgt[...]
        rho = rho_next
        upd[...] = new
        sol_ref[...] = sol_ref[...] + new

    last = SWEEPS
    apply_operator()
    open_faces(last, (img,))

    pressure = sol_ref[...]
    p_high = pressure.astype(jnp.bfloat16)
    rest = pressure - p_high.astype(jnp.float32)
    p_mid = rest.astype(jnp.bfloat16)
    p_low = (rest - p_mid.astype(jnp.float32)).astype(jnp.bfloat16)
    pieces = jnp.concatenate([p_high, p_mid, p_high, p_low], axis=0)
    speed = jnp.zeros((FINE, LANES), jnp.float32)
    for d in range(3):
        slope = jnp.dot(grad[d], pieces, preferred_element_type=jnp.float32)
        value = (trial[d] - slope).astype(jnp.bfloat16)
        vel[d] = value
        for k in range(8):
            wide[64 * d : 64 * d + 64, LANES * k : LANES * (k + 1)] = value[64 * k : 64 * k + 64]
        speed = speed + jnp.abs(value.astype(jnp.float32))
    open_sums(0, 0, jnp.max(speed, axis=0, keepdims=True))

    element = lax.broadcasted_iota(jnp.int32, (LANES, LANES), 0).astype(jnp.float32)
    own_first = (me[0] * LANES).astype(jnp.float32)

    def interpolate(source, target, first, end):
        def lagrange(point):
            value = table_ref[7]
            for j in range(7):
                value = value * (point - table_ref[j])
            return value

        def spread(row):
            row = jnp.broadcast_to(row, (16, LANES)).astype(jnp.bfloat16)
            return jnp.concatenate([row] * (LANES // 16), axis=0)

        def one_tile(i, carry):
            chosen = []
            weights = []
            for h in range(2):
                row = pl.ds(2 * i + h, 1)
                key = source[3, row, :] - own_first
                hot = jnp.where(element == key, 1.0, 0.0).astype(jnp.bfloat16)
                w_x, w_y, w_z = (lagrange(source[axis, row, :]) for axis in range(3))
                weights.append((w_y, w_z))
                chosen.append(
                    jnp.concatenate([hot * spread(w_x[k : k + 1]) for k in range(8)], axis=0)
                )
            taken = jnp.dot(
                wide[...],
                jnp.concatenate(chosen, axis=1),
                preferred_element_type=jnp.float32,
            )
            for d in range(3):
                for h in range(2):
                    part = taken[64 * d : 64 * d + 64, h * LANES : (h + 1) * LANES]
                    w_y, w_z = weights[h]
                    over_y = w_y[0:1] * part[0:8]
                    for l in range(1, 8):
                        over_y = over_y + w_y[l : l + 1] * part[8 * l : 8 * l + 8]
                    target[d, pl.ds(2 * i + h, 1), :] = jnp.sum(
                        w_z * over_y, axis=0, keepdims=True
                    )
            return carry

        lax.fori_loop(first, end, one_tile, 0)

    def finish_faces():
        drain_faces(last - 1)
        close_faces(last, (img,))
        left = res[...] - img[...]
        open_sums(1, 0, jnp.sum(left * left, axis=0, keepdims=True))

    tiles = groups // 2
    half = tiles // 2
    turn = 0
    for offset in order:
        pay_copy(offset).wait_recv()
        for first, end in ((0, half), (half, tiles)):
            interpolate(pay_in.at[offset - 1], back_out.at[offset], first, end)
            if end == tiles:
                back_copy(offset).start()
            turn += 1
            if turn == FINISH:
                finish_faces()
    if turn < FINISH:
        finish_faces()
    interpolate(pay_ref, back_out.at[0], 0, tiles)

    drain_faces(last)
    most = close_sums(0, 0)
    for t in range(1, len(teams)):
        open_sums(0, t, most)
        open_sums(1, t, close_sums(1, t - 1))
        most = close_sums(0, t)
    stride = courant / (jnp.max(most, axis=1, keepdims=True) + 1e-06)
    stride = jnp.broadcast_to(stride, (groups, LANES))
    drain_sums(0)
    for offset in order:
        back_copy(offset).wait_send()
    for offset in order:
        back_copy(offset).wait_recv()
    for d in range(3):
        flow = back_out[0, d]
        for offset in range(1, line):
            flow = flow + back_in[offset - 1, d]
        moved = pay_ref[d] + stride * (1.5 * flow - 0.5 * old_ref[d])
        for g in range(groups):
            flow_ref[d : d + 1, g * LANES : (g + 1) * LANES] = flow[g : g + 1]
            moved_ref[d : d + 1, g * LANES : (g + 1) * LANES] = moved[g : g + 1]

    power_ref[0, 0] = jnp.sum(close_sums(1, len(teams) - 1)) * (
        1.0 / (float(NODES * LANES) * sizes[0] * sizes[1] * sizes[2])
    )
    drain_sums(1)


def write_out(*refs):
    count = (len(refs) - 1) // 2
    sources, targets, given = refs[:count], refs[count : 2 * count], refs[2 * count]
    outward = [pltpu.make_async_copy(sources[i], targets[i], given.at[i]) for i in range(count)]
    for copy in outward:
        copy.start()
    for copy in outward:
        copy.wait()


def per_device(
    sizes,
    element_ops,
    load_terms,
    trial_velocity,
    tracer_coords,
    tracer_old_velocity,
    host_line,
    host_element_index,
):
    count = host_element_index.shape[0]
    groups = count // LANES
    line = sizes[0]
    direct = max(sizes) <= SWEEPS
    seats = sizes[0] * sizes[1] * sizes[2] if direct else sizes[0] + sizes[1] * sizes[2]
    matrix = jnp.asarray(gradient_matrix()).reshape(3, FINE, 4 * NODES)
    f32 = jnp.float32
    i32 = jnp.int32
    bf16 = jnp.bfloat16
    hbm = pl.BlockSpec(memory_space=pltpu.HBM)
    vmem = pl.BlockSpec(memory_space=pltpu.VMEM)
    dma = pltpu.SemaphoreType.DMA
    small = [pltpu.VMEM((NODES, LANES), f32)] * 4
    operands = (
        element_ops,
        load_terms,
        trial_velocity,
        matrix,
        jnp.asarray(weight_table()),
        tracer_coords,
        tracer_old_velocity,
        host_line.reshape(groups, LANES),
        host_element_index.reshape(groups, LANES),
    )
    solution, velocity, power, flows, moved = pl.pallas_call(
        functools.partial(kernel, sizes, direct),
        out_shape=(
            pltpu.VMEM((NODES, LANES), f32),
            pltpu.VMEM((3, FINE, LANES), bf16),
            jax.ShapeDtypeStruct((1, 1), f32),
            pltpu.VMEM((3, count), f32),
            pltpu.VMEM((3, count), f32),
        ),
        in_specs=[hbm] * 9,
        out_specs=(vmem, vmem, pl.BlockSpec(memory_space=pltpu.SMEM), vmem, vmem),
        scratch_shapes=[
            pltpu.VMEM((NODES, NODES, LANES), f32),
            pltpu.VMEM((NODES, LANES), f32),
            pltpu.VMEM((3, FINE, LANES), f32),
            pltpu.VMEM((3, FINE, 4 * NODES), bf16),
            pltpu.VMEM((8, 8, LANES), f32),
            pltpu.VMEM((3, count), f32),
            pltpu.VMEM((3, count), f32),
            pltpu.VMEM((groups, LANES), i32),
            pltpu.VMEM((groups, LANES), i32),
            pltpu.VMEM((4, groups, LANES), f32),
            pltpu.VMEM((3, groups, LANES), f32),
            *small,
            pltpu.VMEM((4, 40, LANES), f32),
            pltpu.VMEM((3 * NODES, 8 * LANES), bf16),
            pltpu.VMEM((SWEEPS + 1, 27, 2 * FACE, LANES), f32),
            pltpu.VMEM((SWEEPS + 1, 27, 2 * FACE, LANES), f32),
            pltpu.VMEM((line - 1, 4, groups, LANES), f32),
            pltpu.VMEM((line, 3, groups, LANES), f32),
            pltpu.VMEM((line - 1, 3, groups, LANES), f32),
            pltpu.VMEM((2, 2, 8, LANES), f32),
            pltpu.VMEM((2, seats, 8, LANES), f32),
            dma((9,)),
            dma((SWEEPS + 1, 27)),
            dma((SWEEPS + 1, 27)),
            dma((line - 1,)),
            dma((line - 1,)),
            dma((line - 1,)),
            dma((line - 1,)),
            dma((2, seats)),
            dma((2, seats)),
        ],
        compiler_params=pltpu.CompilerParams(
            collective_id=0, has_side_effects=True, vmem_limit_bytes=BRICK_VMEM
        ),
        name="brick",
    )(*(pltpu.with_memory_space_constraint(operand, pltpu.HBM) for operand in operands))
    results = (solution, velocity, flows, moved)
    solution, velocity, flows, moved = pl.pallas_call(
        write_out,
        out_shape=tuple(jax.ShapeDtypeStruct(r.shape, r.dtype) for r in results),
        in_specs=[pl.BlockSpec(memory_space=pl.ANY)] * 4,
        out_specs=(hbm,) * 4,
        scratch_shapes=[dma((4,))],
        compiler_params=pltpu.CompilerParams(vmem_limit_bytes=OUT_VMEM),
        name="write_out",
    )(*results)
    return (solution, velocity, power[0, 0], flows, moved)


def solution(mesh):
    sizes = tuple(mesh.shape[axis] for axis in AXES)
    placed = (
        P(None, None, AXES),
        P(None, AXES),
        P(None, None, AXES),
        P(None, AXES),
        P(None, AXES),
        P(AXES, None),
        P(AXES),
    )
    return jax.shard_map(
        functools.partial(per_device, sizes),
        mesh=mesh,
        in_specs=placed,
        out_specs=(
            P(None, AXES),
            P(None, None, AXES),
            P(),
            P(None, AXES),
            P(None, AXES),
        ),
        check_vma=False,
    )
```

```python
import functools

import jax
import jax.numpy as jnp
import numpy as np
from jax import lax
from jax.experimental import pallas as pl
from jax.experimental.pallas import tpu as pltpu
from jax.sharding import PartitionSpec as P

EX = 4
EY = 4
EZ = 8
SWEEPS = 4
NODES = 64
FACE = 16
LANES = 128
FINE = 512

lower_bound = 0.25
upper_bound = 2.0
courant = 0.5
AXES = ("gx", "gy", "gz")
COUNTS = (EX, EY, EZ)
STEPS = (EY * EZ, EZ, 1)
MESH = pl.DeviceIdType.MESH
FINISH = 3
UNROLL = 4
BRICK_VMEM = 24 * 1024 * 1024
OUT_VMEM = 4 * 1024 * 1024


def node_tables():
    coarse = -np.cos(np.pi * np.arange(4) / 3.0)
    fine = -np.cos(np.pi * np.arange(8) / 7.0)
    plain = np.zeros((8, 4))
    slope = np.zeros((8, 4))
    for target in range(8):
        for source in range(4):
            others = [other for other in range(4) if other != source]
            value = 1.0
            for other in others:
                value *= (fine[target] - coarse[other]) / (coarse[source] - coarse[other])
            plain[target, source] = value
            total = 0.0
            for skipped in others:
                term = 1.0 / (coarse[source] - coarse[skipped])
                for other in others:
                    if other != skipped:
                        term *= (fine[target] - coarse[other]) / (coarse[source] - coarse[other])
                total += term
            slope[target, source] = total
    return plain, slope, fine


def gradient_matrix():
    plain, slope, _ = node_tables()
    rows = [
        np.kron(np.kron(slope, plain), plain),
        np.kron(np.kron(plain, slope), plain),
        np.kron(np.kron(plain, plain), slope),
    ]
    full = np.concatenate(rows, axis=0).astype(np.float32)
    high = full.astype(jnp.bfloat16)
    low = (full - high.astype(np.float32)).astype(jnp.bfloat16)
    return np.concatenate([high, high, low, high], axis=1)


def weight_table():
    fine = node_tables()[2]
    table = np.zeros((8, 8, LANES), np.float32)
    for target in range(8):
        others = [other for other in range(8) if other != target]
        scale = 1.0
        for j, other in enumerate(others):
            table[j, target] = fine[other]
            scale /= fine[target] - fine[other]
        table[7, target] = scale
    return table


DIRS = [
    (i, j, k)
    for size in (3, 2, 1)
    for i in (-1, 0, 1)
    for j in (-1, 0, 1)
    for k in (-1, 0, 1)
    if abs(i) + abs(j) + abs(k) == size
]


def slot_of(way):
    return (way[0] + 1) * 9 + (way[1] + 1) * 3 + way[2] + 1


def face_rows(way):
    x, y, z = (None if w == 0 else (3 if w > 0 else 0) for w in way)
    if x is not None and y is not None and z is not None:
        return [(16 * x + 4 * y + z, 1, 1)]
    if x is not None and y is not None:
        return [(16 * x + 4 * y, 4, 1)]
    if x is not None and z is not None:
        return [(16 * x + z, 4, 4)]
    if y is not None and z is not None:
        return [(4 * y + z, 4, 16)]
    if x is not None:
        return [(16 * x, 16, 1)]
    if y is not None:
        return [(16 * a + 4 * y, 4, 1) for a in range(4)]
    return [(z, 16, 4)]


def length_of(way):
    return sum(size for _, size, _ in face_rows(way))


def rows_of(piece):
    start, size, stride = piece
    return (pl.ds(start, size, stride=stride) if stride > 1 else pl.ds(start, size), slice(None))


def bit_moves(size):
    return [1 << bit for bit in range(size.bit_length()) if 1 << bit < size]


def kernel(
    sizes,
    direct,
    ops_hbm,
    load_hbm,
    trial_hbm,
    grad_hbm,
    table_hbm,
    coords_hbm,
    old_hbm,
    line_hbm,
    index_hbm,
    sol_ref,
    vel,
    power_ref,
    flow_ref,
    moved_ref,
    ops,
    load,
    trial,
    grad,
    table_ref,
    coords,
    old,
    host,
    index,
    pay_ref,
    old_ref,
    upd,
    res,
    wgt,
    img,
    work,
    wide,
    face_out,
    face_in,
    pay_in,
    back_out,
    back_in,
    red_out,
    red_in,
    local_sem,
    face_send,
    face_recv,
    pay_send,
    pay_recv,
    back_send,
    back_recv,
    red_send,
    red_recv,
):
    pairs = [
        (ops_hbm, ops),
        (load_hbm, load),
        (line_hbm, host),
        (index_hbm, index),
        (coords_hbm, coords),
        (old_hbm, old),
        (table_hbm, table_ref),
        (trial_hbm, trial),
        (grad_hbm, grad),
    ]
    loads = [
        pltpu.make_async_copy(src, dst, local_sem.at[i]) for i, (src, dst) in enumerate(pairs)
    ]
    for i in (1, 0):
        loads[i].start()

    me = [lax.axis_index(axis) for axis in AXES]
    line = sizes[0]
    groups = pay_ref.shape[1]

    def edge(d, step):
        return me[d] < sizes[d] - 1 if step > 0 else me[d] > 0

    def exists(way):
        tests = [edge(d, way[d]) for d in range(3) if way[d] != 0]
        return functools.reduce(jnp.logical_and, tests)

    present = {way: exists(way) for way in DIRS}

    def beside(way):
        return {AXES[d]: me[d] + way[d] for d in range(3) if way[d] != 0}

    def along(offset):
        there = me[0]
        for bit in bit_moves(line):
            if offset & bit:
                there = there + bit * (1 - 2 * lax.rem(me[0] // bit, 2))
        return {AXES[0]: there}

    def shifted(offset):
        return {
            AXES[d]: lax.rem(me[d] + offset[d], sizes[d]) for d in range(3) if offset[d] != 0
        }

    spans = [range(size) for size in sizes]
    if direct:
        teams = [[(i, j, k) for i in spans[0] for j in spans[1] for k in spans[2]]]
        seats = [(me[0] * sizes[1] + me[1]) * sizes[2] + me[2]]
    else:
        teams = [[(0, j, k) for j in spans[1] for k in spans[2]], [(i, 0, 0) for i in spans[0]]]
        seats = [me[1] * sizes[2] + me[2], me[0]]
    bases = [sum(len(team) for team in teams[:t]) for t in range(len(teams))]

    barrier = pltpu.get_barrier_semaphore()
    for way in DIRS:

        @pl.when(present[way])
        def _():
            pl.semaphore_signal(barrier, inc=1, device_id=beside(way), device_id_type=MESH)

    partners = [along(offset) for offset in range(1, line)]
    if not direct:
        partners += [shifted(offset) for team in teams for offset in team[1:]]
    for partner in partners:
        pl.semaphore_signal(barrier, inc=1, device_id=partner, device_id_type=MESH)

    for copy in loads[2:7]:
        copy.start()

    for way in DIRS:

        @pl.when(jnp.logical_not(present[way]))
        def _():
            for x in range(SWEEPS + 1):
                face_in[x, slot_of(way)] = jnp.zeros((2 * FACE, LANES), jnp.float32)

    lane = lax.broadcasted_iota(jnp.int32, (40, LANES), 1)
    place = [lane // (EY * EZ), lane // EZ % EY, lane % EZ]

    def parts_of(x):
        return 2 if x == 0 else 1

    def face_copy(x, way):
        rows = parts_of(x) * length_of(way)
        there = slot_of(tuple(-w for w in way))
        return pltpu.make_async_remote_copy(
            src_ref=face_out.at[x, slot_of(way), pl.ds(0, rows)],
            dst_ref=face_in.at[x, there, pl.ds(0, rows)],
            send_sem=face_send.at[x, slot_of(way)],
            recv_sem=face_recv.at[x, there],
            device_id=beside(way),
            device_id_type=MESH,
        )

    def fill_faces(x, parts, ways):
        for way in ways:
            at = 0
            for ref in parts:
                for piece in face_rows(way):
                    face_out[x, slot_of(way), at : at + piece[1]] = ref[rows_of(piece)]
                    at += piece[1]

    def start_faces(x, ways):
        for way in ways:

            @pl.when(present[way])
            def _():
                face_copy(x, way).start()

    def drain_faces(x):
        for way in DIRS:

            @pl.when(present[way])
            def _():
                face_copy(x, way).wait_send()

    def open_faces(x, parts):
        for group in (DIRS[:8], DIRS[8:20], DIRS[20:]):
            fill_faces(x, parts, group)
            start_faces(x, group)

    def combine(d, pieces):
        at = 0
        for size, *places in pieces:
            for s, (ref, piece) in enumerate(places):
                work[s, at : at + size] = ref[rows_of(piece)]
            at += size
        count, step = COUNTS[d], STEPS[d]
        far = (count - 1) * step
        total = -(-at // 8) * 8
        low, high, before, after = (work[s, 0:total] for s in range(4))
        where_at = place[d][0:total]
        new = (
            low
            + jnp.where(
                where_at > 0,
                pltpu.roll(high, step, 1),
                pltpu.roll(before, (LANES - far) % LANES, 1),
            ),
            high
            + jnp.where(
                where_at < count - 1,
                pltpu.roll(low, LANES - step, 1),
                pltpu.roll(after, far, 1),
            ),
        )
        at = 0
        for size, *places in pieces:
            for s in range(2):
                ref, piece = places[s]
                ref[rows_of(piece)] = new[s][at : at + size]
            at += size

    def close_faces(x, parts):
        for way in DIRS:

            @pl.when(present[way])
            def _():
                face_copy(x, tuple(-w for w in way)).wait_recv()

        ends = (-1, 1)
        for p, ref in enumerate(parts):

            def got(way, start=0, size=None, stride=1):
                full = length_of(way)
                return (
                    face_in.at[x, slot_of(way)],
                    (p * full + start, full if size is None else size, stride),
                )

            pieces = [(16, (ref, (0, 16, 1)), (ref, (48, 16, 1)), got((-1, 0, 0)), got((1, 0, 0)))]
            for o in ends:
                for way in ((0, o, 0), (0, 0, o)):
                    lo, hi = (-1, *way[1:]), (1, *way[1:])
                    pieces.append((4, got(way, 0, 4), got(way, 12, 4), got(lo), got(hi)))
            for oy in ends:
                for oz in ends:
                    way = (0, oy, oz)
                    pieces.append(
                        (1, got(way, 0, 1), got(way, 3, 1), got((-1, oy, oz)), got((1, oy, oz)))
                    )
            combine(0, pieces)
            pieces = []
            for a in range(4):
                pieces.append(
                    (
                        4,
                        (ref, (16 * a, 4, 1)),
                        (ref, (16 * a + 12, 4, 1)),
                        got((0, -1, 0), 4 * a, 4),
                        got((0, 1, 0), 4 * a, 4),
                    )
                )
            for oz in ends:
                way = (0, 0, oz)
                pieces.append(
                    (4, got(way, 0, 4, 4), got(way, 3, 4, 4), got((0, -1, oz)), got((0, 1, oz)))
                )
            combine(1, pieces)
            combine(
                2,
                [(16, (ref, (0, 16, 4)), (ref, (3, 16, 4)), got((0, 0, -1)), got((0, 0, 1)))],
            )

    def apply_operator():
        def block(i, total):
            rows = upd[pl.ds(pl.multiple_of(8 * i, 8), 8), :]
            for j in range(8):
                total = total + ops[8 * i + j] * rows[j : j + 1, :]
            return total

        img[...] = lax.fori_loop(0, NODES // 8, block, jnp.zeros((NODES, LANES), jnp.float32))

    def pay_copy(offset):
        return pltpu.make_async_remote_copy(
            src_ref=pay_ref,
            dst_ref=pay_in.at[offset - 1],
            send_sem=pay_send.at[offset - 1],
            recv_sem=pay_recv.at[offset - 1],
            device_id=along(offset),
            device_id_type=MESH,
        )

    def back_copy(offset):
        return pltpu.make_async_remote_copy(
            src_ref=back_out.at[offset],
            dst_ref=back_in.at[offset - 1],
            send_sem=back_send.at[offset - 1],
            recv_sem=back_recv.at[offset - 1],
            device_id=along(offset),
            device_id_type=MESH,
        )

    def red_copy(kind, t, offset):
        return pltpu.make_async_remote_copy(
            src_ref=red_out.at[kind, t, pl.ds(0, 1)],
            dst_ref=red_in.at[kind, bases[t] + seats[t], pl.ds(0, 1)],
            send_sem=red_send.at[kind, bases[t] + offset],
            recv_sem=red_recv.at[kind, bases[t] + offset],
            device_id=shifted(teams[t][offset]),
            device_id_type=MESH,
        )

    def open_sums(kind, t, value):
        red_out[kind, t, 0:1] = value
        for offset in range(len(teams[t]) - 1, 0, -1):
            red_copy(kind, t, offset).start()
        red_in[kind, bases[t] + seats[t], 0:1] = value

    def close_sums(kind, t):
        for offset in range(1, len(teams[t])):
            red_copy(kind, t, offset).wait_recv()
        values = [red_in[kind, bases[t] + i, 0:1] for i in range(len(teams[t]))]
        join = jnp.add if kind else jnp.maximum
        while len(values) > 1:
            values = [
                join(*values[i : i + 2]) if i + 1 < len(values) else values[i]
                for i in range(0, len(values), 2)
            ]
        return values[0]

    def drain_sums(kind):
        for t, team in enumerate(teams):
            for offset in range(1, len(team)):
                red_copy(kind, t, offset).wait_send()

    loads[1].wait()
    loads[0].wait()
    res[...] = load[...]
    for n in range(NODES):
        wgt[n : n + 1, :] = ops[n, n : n + 1, :]
    fill_faces(0, (res, wgt), DIRS)
    for copy in loads[2:7]:
        copy.wait()
    pay_ref[3] = (host[...] * LANES + index[...]).astype(jnp.float32)
    for d in range(3):
        for g in range(groups):
            lanes = slice(g * LANES, (g + 1) * LANES)
            pay_ref[d, g : g + 1, :] = coords[d : d + 1, lanes]
            old_ref[d, g : g + 1, :] = old[d : d + 1, lanes]

    near = [sum(edge(d, step).astype(jnp.int32) for step in (-1, 1)) for d in range(3)]
    pl.semaphore_wait(
        barrier, len(partners) + (1 + near[0]) * (1 + near[1]) * (1 + near[2]) - 1
    )

    start_faces(0, DIRS)
    order = range(line - 1, 0, -1)
    for offset in order:
        pay_copy(offset).start()
    for copy in loads[7:]:
        copy.start()
    close_faces(0, (res, wgt))

    center = 0.5 * (upper_bound + lower_bound)
    radius = 0.5 * (upper_bound - lower_bound)
    sigma = center / radius
    rho = 1.0 / sigma
    upd[...] = res[...] / (center * wgt[...])
    sol_ref[...] = upd[...]
    for sweep in range(SWEEPS - 1):
        apply_operator()
        open_faces(sweep + 1, (img,))
        drain_faces(sweep)
        if sweep + 2 == SWEEPS:
            for copy in loads[7:]:
                copy.wait()
            for offset in order:
                pay_copy(offset).wait_send()
        close_faces(sweep + 1, (img,))
        left = res[...] - img[...]
        res[...] = left
        rho_next = 1.0 / (2.0 * sigma - rho)
        new = (rho_next * rho) * upd[...] + (2.0 * rho_next / radius) * left / wgt[...]
        rho = rho_next
        upd[...] = new
        sol_ref[...] = sol_ref[...] + new

    last = SWEEPS
    apply_operator()
    open_faces(last, (img,))

    pressure = sol_ref[...]
    p_high = pressure.astype(jnp.bfloat16)
    rest = pressure - p_high.astype(jnp.float32)
    p_mid = rest.astype(jnp.bfloat16)
    p_low = (rest - p_mid.astype(jnp.float32)).astype(jnp.bfloat16)
    pieces = jnp.concatenate([p_high, p_mid, p_high, p_low], axis=0)
    speed = jnp.zeros((FINE, LANES), jnp.float32)
    for d in range(3):
        slope = jnp.dot(grad[d], pieces, preferred_element_type=jnp.float32)
        value = (trial[d] - slope).astype(jnp.bfloat16)
        vel[d] = value
        for k in range(8):
            wide[64 * d : 64 * d + 64, LANES * k : LANES * (k + 1)] = value[64 * k : 64 * k + 64]
        speed = speed + jnp.abs(value.astype(jnp.float32))
    open_sums(0, 0, jnp.max(speed, axis=0, keepdims=True))

    element = lax.broadcasted_iota(jnp.int32, (LANES, LANES), 0).astype(jnp.float32)
    own_first = (me[0] * LANES).astype(jnp.float32)

    def interpolate(source, target, first, end):
        def lagrange(point):
            value = table_ref[7]
            for j in range(7):
                value = value * (point - table_ref[j])
            return value

        def spread(row):
            row = jnp.broadcast_to(row, (16, LANES)).astype(jnp.bfloat16)
            return jnp.concatenate([row] * (LANES // 16), axis=0)

        def one_tile(i, carry):
            chosen = []
            weights = []
            for h in range(2):
                row = pl.ds(2 * i + h, 1)
                key = source[3, row, :] - own_first
                hot = jnp.where(element == key, 1.0, 0.0).astype(jnp.bfloat16)
                w_x, w_y, w_z = (lagrange(source[axis, row, :]) for axis in range(3))
                weights.append((w_y, w_z))
                chosen.append(
                    jnp.concatenate([hot * spread(w_x[k : k + 1]) for k in range(8)], axis=0)
                )
            taken = jnp.dot(
                wide[...],
                jnp.concatenate(chosen, axis=1),
                preferred_element_type=jnp.float32,
            )
            for d in range(3):
                for h in range(2):
                    part = taken[64 * d : 64 * d + 64, h * LANES : (h + 1) * LANES]
                    w_y, w_z = weights[h]
                    over_y = w_y[0:1] * part[0:8]
                    for l in range(1, 8):
                        over_y = over_y + w_y[l : l + 1] * part[8 * l : 8 * l + 8]
                    target[d, pl.ds(2 * i + h, 1), :] = jnp.sum(
                        w_z * over_y, axis=0, keepdims=True
                    )
            return carry

        lax.fori_loop(first, end, one_tile, 0, unroll=UNROLL)

    def finish_faces():
        drain_faces(last - 1)
        close_faces(last, (img,))
        left = res[...] - img[...]
        open_sums(1, 0, jnp.sum(left * left, axis=0, keepdims=True))

    tiles = groups // 2
    half = tiles // 2
    turn = 0
    for offset in order:
        pay_copy(offset).wait_recv()
        for first, end in ((0, half), (half, tiles)):
            interpolate(pay_in.at[offset - 1], back_out.at[offset], first, end)
            if end == tiles:
                back_copy(offset).start()
            turn += 1
            if turn == FINISH:
                finish_faces()
    if turn < FINISH:
        finish_faces()
    interpolate(pay_ref, back_out.at[0], 0, tiles)

    drain_faces(last)
    most = close_sums(0, 0)
    for t in range(1, len(teams)):
        open_sums(0, t, most)
        open_sums(1, t, close_sums(1, t - 1))
        most = close_sums(0, t)
    stride = courant / (jnp.max(most, axis=1, keepdims=True) + 1e-06)
    stride = jnp.broadcast_to(stride, (groups, LANES))
    drain_sums(0)
    for offset in order:
        back_copy(offset).wait_send()
    for offset in order:
        back_copy(offset).wait_recv()
    for d in range(3):
        flow = back_out[0, d]
        for offset in range(1, line):
            flow = flow + back_in[offset - 1, d]
        moved = pay_ref[d] + stride * (1.5 * flow - 0.5 * old_ref[d])
        for g in range(groups):
            flow_ref[d : d + 1, g * LANES : (g + 1) * LANES] = flow[g : g + 1]
            moved_ref[d : d + 1, g * LANES : (g + 1) * LANES] = moved[g : g + 1]

    drain_sums(1)
    total = jnp.sum(close_sums(1, len(teams) - 1), axis=1, keepdims=True)
    power_ref[...] = jnp.broadcast_to(
        total * (1.0 / (float(NODES * LANES) * sizes[0] * sizes[1] * sizes[2])), (8, LANES)
    )


def write_out(*refs):
    count = (len(refs) - 2) // 2
    sources, targets = refs[:count], refs[count : 2 * count]
    held, given = refs[2 * count :]
    outward = [pltpu.make_async_copy(sources[i], targets[i], given.at[i]) for i in range(1, count)]
    outward.append(pltpu.make_async_copy(held, targets[0], given.at[0]))
    for copy in outward[:-1]:
        copy.start()
    held[0, 0] = sources[0][0, 0]
    outward[-1].start()
    for copy in outward:
        copy.wait()


def per_device(
    sizes,
    element_ops,
    load_terms,
    trial_velocity,
    tracer_coords,
    tracer_old_velocity,
    host_line,
    host_element_index,
):
    count = host_element_index.shape[0]
    groups = count // LANES
    line = sizes[0]
    direct = max(sizes) <= SWEEPS
    seats = sizes[0] * sizes[1] * sizes[2] if direct else sizes[0] + sizes[1] * sizes[2]
    matrix = jnp.asarray(gradient_matrix()).reshape(3, FINE, 4 * NODES)
    f32 = jnp.float32
    i32 = jnp.int32
    bf16 = jnp.bfloat16
    hbm = pl.BlockSpec(memory_space=pltpu.HBM)
    vmem = pl.BlockSpec(memory_space=pltpu.VMEM)
    dma = pltpu.SemaphoreType.DMA
    small = [pltpu.VMEM((NODES, LANES), f32)] * 4
    operands = (
        element_ops,
        load_terms,
        trial_velocity,
        matrix,
        jnp.asarray(weight_table()),
        tracer_coords,
        tracer_old_velocity,
        host_line.reshape(groups, LANES),
        host_element_index.reshape(groups, LANES),
    )
    solution, velocity, power, flows, moved = pl.pallas_call(
        functools.partial(kernel, sizes, direct),
        out_shape=(
            pltpu.VMEM((NODES, LANES), f32),
            pltpu.VMEM((3, FINE, LANES), bf16),
            pltpu.VMEM((8, LANES), f32),
            pltpu.VMEM((3, count), f32),
            pltpu.VMEM((3, count), f32),
        ),
        in_specs=[hbm] * 9,
        out_specs=(vmem,) * 5,
        scratch_shapes=[
            pltpu.VMEM((NODES, NODES, LANES), f32),
            pltpu.VMEM((NODES, LANES), f32),
            pltpu.VMEM((3, FINE, LANES), f32),
            pltpu.VMEM((3, FINE, 4 * NODES), bf16),
            pltpu.VMEM((8, 8, LANES), f32),
            pltpu.VMEM((3, count), f32),
            pltpu.VMEM((3, count), f32),
            pltpu.VMEM((groups, LANES), i32),
            pltpu.VMEM((groups, LANES), i32),
            pltpu.VMEM((4, groups, LANES), f32),
            pltpu.VMEM((3, groups, LANES), f32),
            *small,
            pltpu.VMEM((4, 40, LANES), f32),
            pltpu.VMEM((3 * NODES, 8 * LANES), bf16),
            pltpu.VMEM((SWEEPS + 1, 27, 2 * FACE, LANES), f32),
            pltpu.VMEM((SWEEPS + 1, 27, 2 * FACE, LANES), f32),
            pltpu.VMEM((line - 1, 4, groups, LANES), f32),
            pltpu.VMEM((line, 3, groups, LANES), f32),
            pltpu.VMEM((line - 1, 3, groups, LANES), f32),
            pltpu.VMEM((2, 2, 8, LANES), f32),
            pltpu.VMEM((2, seats, 8, LANES), f32),
            dma((9,)),
            dma((SWEEPS + 1, 27)),
            dma((SWEEPS + 1, 27)),
            dma((line - 1,)),
            dma((line - 1,)),
            dma((line - 1,)),
            dma((line - 1,)),
            dma((2, seats)),
            dma((2, seats)),
        ],
        compiler_params=pltpu.CompilerParams(
            collective_id=0, has_side_effects=True, vmem_limit_bytes=BRICK_VMEM
        ),
        name="brick",
    )(*(pltpu.with_memory_space_constraint(operand, pltpu.HBM) for operand in operands))
    results = (power, solution, velocity, flows, moved)
    shapes = ((1, 1),) + tuple(r.shape for r in results[1:])
    power, solution, velocity, flows, moved = pl.pallas_call(
        write_out,
        out_shape=tuple(jax.ShapeDtypeStruct(z, r.dtype) for z, r in zip(shapes, results)),
        in_specs=[vmem] + [pl.BlockSpec(memory_space=pl.ANY)] * 4,
        out_specs=(hbm,) * 5,
        scratch_shapes=[pltpu.SMEM((1, 1), f32), dma((5,))],
        compiler_params=pltpu.CompilerParams(vmem_limit_bytes=OUT_VMEM),
        name="write_out",
    )(*results)
    return (solution, velocity, power.reshape(()), flows, moved)


def solution(mesh):
    sizes = tuple(mesh.shape[axis] for axis in AXES)
    placed = (
        P(None, None, AXES),
        P(None, AXES),
        P(None, None, AXES),
        P(None, AXES),
        P(None, AXES),
        P(AXES, None),
        P(AXES),
    )
    return jax.shard_map(
        functools.partial(per_device, sizes),
        mesh=mesh,
        in_specs=placed,
        out_specs=(
            P(None, AXES),
            P(None, None, AXES),
            P(),
            P(None, AXES),
            P(None, AXES),
        ),
        check_vma=False,
    )
```

```python
import functools

import jax
import jax.numpy as jnp
import numpy as np
from jax import lax
from jax.experimental import pallas as pl
from jax.experimental.pallas import tpu as pltpu
from jax.sharding import PartitionSpec as P

EX = 4
EY = 4
EZ = 8
SWEEPS = 4
NODES = 64
FACE = 16
LANES = 128
FINE = 512

lower_bound = 0.25
upper_bound = 2.0
courant = 0.5
AXES = ("gx", "gy", "gz")
COUNTS = (EX, EY, EZ)
STEPS = (EY * EZ, EZ, 1)
MESH = pl.DeviceIdType.MESH
FINISH = 3
UNROLL = 4
PAY_SWEEP = 1
SPLIT = 8
BRICK_VMEM = 24 * 1024 * 1024
OUT_VMEM = 4 * 1024 * 1024


def node_tables():
    coarse = -np.cos(np.pi * np.arange(4) / 3.0)
    fine = -np.cos(np.pi * np.arange(8) / 7.0)
    plain = np.zeros((8, 4))
    slope = np.zeros((8, 4))
    for target in range(8):
        for source in range(4):
            others = [other for other in range(4) if other != source]
            value = 1.0
            for other in others:
                value *= (fine[target] - coarse[other]) / (coarse[source] - coarse[other])
            plain[target, source] = value
            total = 0.0
            for skipped in others:
                term = 1.0 / (coarse[source] - coarse[skipped])
                for other in others:
                    if other != skipped:
                        term *= (fine[target] - coarse[other]) / (coarse[source] - coarse[other])
                total += term
            slope[target, source] = total
    return plain, slope, fine


def gradient_matrix():
    plain, slope, _ = node_tables()
    rows = [
        np.kron(np.kron(slope, plain), plain),
        np.kron(np.kron(plain, slope), plain),
        np.kron(np.kron(plain, plain), slope),
    ]
    full = np.concatenate(rows, axis=0).astype(np.float32)
    high = full.astype(jnp.bfloat16)
    low = (full - high.astype(np.float32)).astype(jnp.bfloat16)
    return np.concatenate([high, high, low, high], axis=1)


def weight_table():
    fine = node_tables()[2]
    table = np.zeros((8, 8, LANES), np.float32)
    for target in range(8):
        others = [other for other in range(8) if other != target]
        scale = 1.0
        for j, other in enumerate(others):
            table[j, target] = fine[other]
            scale /= fine[target] - fine[other]
        table[7, target] = scale
    return table


DIRS = [
    (i, j, k)
    for size in (3, 2, 1)
    for i in (-1, 0, 1)
    for j in (-1, 0, 1)
    for k in (-1, 0, 1)
    if abs(i) + abs(j) + abs(k) == size
]


def slot_of(way):
    return (way[0] + 1) * 9 + (way[1] + 1) * 3 + way[2] + 1


def face_rows(way):
    x, y, z = (None if w == 0 else (3 if w > 0 else 0) for w in way)
    if x is not None and y is not None and z is not None:
        return [(16 * x + 4 * y + z, 1, 1)]
    if x is not None and y is not None:
        return [(16 * x + 4 * y, 4, 1)]
    if x is not None and z is not None:
        return [(16 * x + z, 4, 4)]
    if y is not None and z is not None:
        return [(4 * y + z, 4, 16)]
    if x is not None:
        return [(16 * x, 16, 1)]
    if y is not None:
        return [(16 * a + 4 * y, 4, 1) for a in range(4)]
    return [(z, 16, 4)]


def length_of(way):
    return sum(size for _, size, _ in face_rows(way))


def rows_of(piece):
    start, size, stride = piece
    return (pl.ds(start, size, stride=stride) if stride > 1 else pl.ds(start, size), slice(None))


def bit_moves(size):
    return [1 << bit for bit in range(size.bit_length()) if 1 << bit < size]


def kernel(
    sizes,
    direct,
    ops_hbm,
    load_hbm,
    trial_hbm,
    grad_hbm,
    table_hbm,
    coords_hbm,
    old_hbm,
    line_hbm,
    index_hbm,
    sol_ref,
    vel,
    power_ref,
    flow_ref,
    moved_ref,
    ops,
    load,
    trial,
    grad,
    table_ref,
    coords,
    old,
    host,
    index,
    pay_ref,
    old_ref,
    upd,
    res,
    wgt,
    img,
    work,
    wide,
    diag,
    face_out,
    face_in,
    pay_in,
    back_out,
    back_in,
    red_out,
    red_in,
    local_sem,
    face_send,
    face_recv,
    pay_send,
    pay_recv,
    back_send,
    back_recv,
    red_send,
    red_recv,
):
    pairs = [
        (ops_hbm, ops),
        (load_hbm, load),
        (line_hbm, host),
        (index_hbm, index),
        (coords_hbm, coords),
        (old_hbm, old),
        (table_hbm, table_ref),
        (trial_hbm, trial),
        (grad_hbm, grad),
    ]
    loads = [
        pltpu.make_async_copy(src, dst, local_sem.at[i]) for i, (src, dst) in enumerate(pairs)
    ]
    corners = [
        pltpu.make_async_copy(
            ops_hbm.at[pl.ds(n, 8), pl.ds(n, 8)], diag.at[n // 8], local_sem.at[9]
        )
        for n in range(0, NODES, 8)
    ]
    loads[1].start()
    for copy in corners:
        copy.start()
    loads[0].start()

    me = [lax.axis_index(axis) for axis in AXES]
    line = sizes[0]
    groups = pay_ref.shape[1]

    def edge(d, step):
        return me[d] < sizes[d] - 1 if step > 0 else me[d] > 0

    def exists(way):
        tests = [edge(d, way[d]) for d in range(3) if way[d] != 0]
        return functools.reduce(jnp.logical_and, tests)

    present = {way: exists(way) for way in DIRS}

    def beside(way):
        return {AXES[d]: me[d] + way[d] for d in range(3) if way[d] != 0}

    def along(offset):
        there = me[0]
        for bit in bit_moves(line):
            if offset & bit:
                there = there + bit * (1 - 2 * lax.rem(me[0] // bit, 2))
        return {AXES[0]: there}

    def shifted(offset):
        return {
            AXES[d]: lax.rem(me[d] + offset[d], sizes[d]) for d in range(3) if offset[d] != 0
        }

    spans = [range(size) for size in sizes]
    if direct:
        teams = [[(i, j, k) for i in spans[0] for j in spans[1] for k in spans[2]]]
        seats = [(me[0] * sizes[1] + me[1]) * sizes[2] + me[2]]
    else:
        teams = [[(0, j, k) for j in spans[1] for k in spans[2]], [(i, 0, 0) for i in spans[0]]]
        seats = [me[1] * sizes[2] + me[2], me[0]]
    bases = [sum(len(team) for team in teams[:t]) for t in range(len(teams))]

    barrier = pltpu.get_barrier_semaphore()
    held = [
        {w: jnp.clip(me[d] + w, 0, sizes[d] - 1) for w in (-1, 0, 1)} for d in range(3)
    ]
    for way in DIRS:
        near = {AXES[d]: held[d][way[d]] for d in range(3) if way[d] != 0}
        pl.semaphore_signal(barrier, inc=1, device_id=near, device_id_type=MESH)

    partners = [along(offset) for offset in range(1, line)]
    if not direct:
        partners += [shifted(offset) for team in teams for offset in team[1:]]
    for partner in partners:
        pl.semaphore_signal(barrier, inc=1, device_id=partner, device_id_type=MESH)

    for copy in loads[2:7]:
        copy.start()

    for way in DIRS:

        @pl.when(jnp.logical_not(present[way]))
        def _():
            for x in range(SWEEPS + 1):
                face_in[x, slot_of(way)] = jnp.zeros((2 * FACE, LANES), jnp.float32)

    lane = lax.broadcasted_iota(jnp.int32, (40, LANES), 1)
    place = [lane // (EY * EZ), lane // EZ % EY, lane % EZ]

    def parts_of(x):
        return 2 if x == 0 else 1

    def face_copy(x, way):
        rows = parts_of(x) * length_of(way)
        there = slot_of(tuple(-w for w in way))
        return pltpu.make_async_remote_copy(
            src_ref=face_out.at[x, slot_of(way), pl.ds(0, rows)],
            dst_ref=face_in.at[x, there, pl.ds(0, rows)],
            send_sem=face_send.at[x % 2, slot_of(way)],
            recv_sem=face_recv.at[x % 2, there],
            device_id=beside(way),
            device_id_type=MESH,
        )

    def fill_faces(x, parts, ways):
        for way in ways:
            at = 0
            for ref in parts:
                for piece in face_rows(way):
                    face_out[x, slot_of(way), at : at + piece[1]] = ref[rows_of(piece)]
                    at += piece[1]

    def start_faces(x, ways):
        for way in ways:

            @pl.when(present[way])
            def _():
                face_copy(x, way).start()

    def drain_faces(x):
        for way in DIRS:

            @pl.when(present[way])
            def _():
                face_copy(x, way).wait_send()

    def open_faces(x, parts):
        for group in (DIRS[:8], DIRS[8:20], DIRS[20:]):
            fill_faces(x, parts, group)
            start_faces(x, group)

    def combine(d, pieces):
        at = 0
        for size, *places in pieces:
            for s, (ref, piece) in enumerate(places):
                work[s, at : at + size] = ref[rows_of(piece)]
            at += size
        count, step = COUNTS[d], STEPS[d]
        far = (count - 1) * step
        total = -(-at // 8) * 8
        low, high, before, after = (work[s, 0:total] for s in range(4))
        where_at = place[d][0:total]
        new = (
            low
            + jnp.where(
                where_at > 0,
                pltpu.roll(high, step, 1),
                pltpu.roll(before, (LANES - far) % LANES, 1),
            ),
            high
            + jnp.where(
                where_at < count - 1,
                pltpu.roll(low, LANES - step, 1),
                pltpu.roll(after, far, 1),
            ),
        )
        at = 0
        for size, *places in pieces:
            for s in range(2):
                ref, piece = places[s]
                ref[rows_of(piece)] = new[s][at : at + size]
            at += size

    def close_faces(x, parts):
        for way in DIRS[::-1]:

            @pl.when(present[way])
            def _():
                face_copy(x, tuple(-w for w in way)).wait_recv()

        ends = (-1, 1)
        for p, ref in enumerate(parts):

            def got(way, start=0, size=None, stride=1):
                full = length_of(way)
                return (
                    face_in.at[x, slot_of(way)],
                    (p * full + start, full if size is None else size, stride),
                )

            pieces = [(16, (ref, (0, 16, 1)), (ref, (48, 16, 1)), got((-1, 0, 0)), got((1, 0, 0)))]
            for o in ends:
                for way in ((0, o, 0), (0, 0, o)):
                    lo, hi = (-1, *way[1:]), (1, *way[1:])
                    pieces.append((4, got(way, 0, 4), got(way, 12, 4), got(lo), got(hi)))
            for oy in ends:
                for oz in ends:
                    way = (0, oy, oz)
                    pieces.append(
                        (1, got(way, 0, 1), got(way, 3, 1), got((-1, oy, oz)), got((1, oy, oz)))
                    )
            combine(0, pieces)
            pieces = []
            for a in range(4):
                pieces.append(
                    (
                        4,
                        (ref, (16 * a, 4, 1)),
                        (ref, (16 * a + 12, 4, 1)),
                        got((0, -1, 0), 4 * a, 4),
                        got((0, 1, 0), 4 * a, 4),
                    )
                )
            for oz in ends:
                way = (0, 0, oz)
                pieces.append(
                    (4, got(way, 0, 4, 4), got(way, 3, 4, 4), got((0, -1, oz)), got((0, 1, oz)))
                )
            combine(1, pieces)
            combine(
                2,
                [(16, (ref, (0, 16, 4)), (ref, (3, 16, 4)), got((0, 0, -1)), got((0, 0, 1)))],
            )

    def apply_operator():
        def block(i, total):
            rows = upd[pl.ds(pl.multiple_of(8 * i, 8), 8), :]
            for j in range(8):
                total = total + ops[8 * i + j] * rows[j : j + 1, :]
            return total

        img[...] = lax.fori_loop(0, NODES // 8, block, jnp.zeros((NODES, LANES), jnp.float32), unroll=SPLIT)

    def settle(view, sem):
        pltpu.make_async_copy(view, view, sem).wait()

    def pay_copy(offset):
        return pltpu.make_async_remote_copy(
            src_ref=pay_ref,
            dst_ref=pay_in.at[offset - 1],
            send_sem=pay_send.at[0],
            recv_sem=pay_recv.at[offset - 1],
            device_id=along(offset),
            device_id_type=MESH,
        )

    def back_copy(offset):
        return pltpu.make_async_remote_copy(
            src_ref=back_out.at[offset],
            dst_ref=back_in.at[offset - 1],
            send_sem=back_send.at[0],
            recv_sem=back_recv.at[0],
            device_id=along(offset),
            device_id_type=MESH,
        )

    def red_copy(kind, t, offset):
        return pltpu.make_async_remote_copy(
            src_ref=red_out.at[kind, t, pl.ds(0, 1)],
            dst_ref=red_in.at[kind, bases[t] + seats[t], pl.ds(0, 1)],
            send_sem=red_send.at[kind, t],
            recv_sem=red_recv.at[kind, t],
            device_id=shifted(teams[t][offset]),
            device_id_type=MESH,
        )

    def others(kind, t):
        return red_in.at[kind, pl.ds(bases[t], len(teams[t]) - 1), pl.ds(0, 1)]

    def open_sums(kind, t, value):
        red_out[kind, t, 0:1] = value
        for offset in range(len(teams[t]) - 1, 0, -1):
            red_copy(kind, t, offset).start()
        red_in[kind, bases[t] + seats[t], 0:1] = value

    def close_sums(kind, t):
        settle(others(kind, t), red_recv.at[kind, t])
        values = [red_in[kind, bases[t] + i, 0:1] for i in range(len(teams[t]))]
        join = jnp.add if kind else jnp.maximum
        while len(values) > 1:
            values = [
                join(*values[i : i + 2]) if i + 1 < len(values) else values[i]
                for i in range(0, len(values), 2)
            ]
        return values[0]

    def drain_sums(kind):
        for t in range(len(teams)):
            settle(others(kind, t), red_send.at[kind, t])

    loads[1].wait()
    settle(ops.at[pl.ds(0, 8)], local_sem.at[9])
    res[...] = load[...]
    for n in range(NODES):
        wgt[n : n + 1, :] = diag[n // 8, n % 8, n % 8 : n % 8 + 1, :]
    fill_faces(0, (res, wgt), DIRS)
    pl.semaphore_wait(barrier, len(partners) + len(DIRS))

    start_faces(0, DIRS)
    for copy in loads[2:7]:
        copy.wait()
    pay_ref[3] = (host[...] * LANES + index[...]).astype(jnp.float32)
    for d in range(3):
        for g in range(groups):
            lanes = slice(g * LANES, (g + 1) * LANES)
            pay_ref[d, g : g + 1, :] = coords[d : d + 1, lanes]
            old_ref[d, g : g + 1, :] = old[d : d + 1, lanes]
    order = range(line - 1, 0, -1)
    for copy in loads[7:]:
        copy.start()
    close_faces(0, (res, wgt))

    loads[0].wait()
    center = 0.5 * (upper_bound + lower_bound)
    radius = 0.5 * (upper_bound - lower_bound)
    sigma = center / radius
    rho = 1.0 / sigma
    upd[...] = res[...] / (center * wgt[...])
    sol_ref[...] = upd[...]
    for sweep in range(SWEEPS - 1):
        apply_operator()
        open_faces(sweep + 1, (img,))
        if sweep == PAY_SWEEP:
            for offset in order:
                pay_copy(offset).start()
        drain_faces(sweep)
        if sweep + 2 == SWEEPS:
            for copy in loads[7:]:
                copy.wait()
            settle(pay_in, pay_send.at[0])
        close_faces(sweep + 1, (img,))
        left = res[...] - img[...]
        res[...] = left
        rho_next = 1.0 / (2.0 * sigma - rho)
        new = (rho_next * rho) * upd[...] + (2.0 * rho_next / radius) * left / wgt[...]
        rho = rho_next
        upd[...] = new
        sol_ref[...] = sol_ref[...] + new

    last = SWEEPS
    apply_operator()
    open_faces(last, (img,))

    pressure = sol_ref[...]
    p_high = pressure.astype(jnp.bfloat16)
    rest = pressure - p_high.astype(jnp.float32)
    p_mid = rest.astype(jnp.bfloat16)
    p_low = (rest - p_mid.astype(jnp.float32)).astype(jnp.bfloat16)
    pieces = jnp.concatenate([p_high, p_mid, p_high, p_low], axis=0)
    speed = jnp.zeros((FINE, LANES), jnp.float32)
    for d in range(3):
        slope = jnp.dot(grad[d], pieces, preferred_element_type=jnp.float32)
        value = (trial[d] - slope).astype(jnp.bfloat16)
        vel[d] = value
        for k in range(8):
            wide[64 * d : 64 * d + 64, LANES * k : LANES * (k + 1)] = value[64 * k : 64 * k + 64]
        speed = speed + jnp.abs(value.astype(jnp.float32))
    open_sums(0, 0, jnp.max(speed, axis=0, keepdims=True))

    element = lax.broadcasted_iota(jnp.int32, (LANES, LANES), 0).astype(jnp.float32)
    own_first = (me[0] * LANES).astype(jnp.float32)

    def interpolate(source, target, first, end):
        def lagrange(point):
            value = table_ref[7]
            for j in range(7):
                value = value * (point - table_ref[j])
            return value

        def spread(row):
            row = jnp.broadcast_to(row, (16, LANES)).astype(jnp.bfloat16)
            return jnp.concatenate([row] * (LANES // 16), axis=0)

        def one_tile(i, carry):
            chosen = []
            weights = []
            for h in range(2):
                row = pl.ds(2 * i + h, 1)
                key = source[3, row, :] - own_first
                hot = jnp.where(element == key, 1.0, 0.0).astype(jnp.bfloat16)
                w_x, w_y, w_z = (lagrange(source[axis, row, :]) for axis in range(3))
                weights.append((w_y, w_z))
                chosen.append(
                    jnp.concatenate([hot * spread(w_x[k : k + 1]) for k in range(8)], axis=0)
                )
            taken = jnp.dot(
                wide[...],
                jnp.concatenate(chosen, axis=1),
                preferred_element_type=jnp.float32,
            )
            for d in range(3):
                for h in range(2):
                    part = taken[64 * d : 64 * d + 64, h * LANES : (h + 1) * LANES]
                    w_y, w_z = weights[h]
                    over_y = w_y[0:1] * part[0:8]
                    for l in range(1, 8):
                        over_y = over_y + w_y[l : l + 1] * part[8 * l : 8 * l + 8]
                    target[d, pl.ds(2 * i + h, 1), :] = jnp.sum(
                        w_z * over_y, axis=0, keepdims=True
                    )
            return carry

        lax.fori_loop(first, end, one_tile, 0, unroll=UNROLL)

    def finish_faces():
        drain_faces(last - 1)
        close_faces(last, (img,))
        left = res[...] - img[...]
        open_sums(1, 0, jnp.sum(left * left, axis=0, keepdims=True))

    tiles = groups // 2
    half = tiles // 2
    turn = 0
    for offset in order:
        pay_copy(offset).wait_recv()
        for first, end in ((0, half), (half, tiles)):
            interpolate(pay_in.at[offset - 1], back_out.at[offset], first, end)
            if end == tiles:
                back_copy(offset).start()
            turn += 1
            if turn == FINISH:
                finish_faces()
    if turn < FINISH:
        finish_faces()
    interpolate(pay_ref, back_out.at[0], 0, tiles)

    drain_faces(last)
    most = close_sums(0, 0)
    for t in range(1, len(teams)):
        open_sums(0, t, most)
        open_sums(1, t, close_sums(1, t - 1))
        most = close_sums(0, t)
    stride = courant / (jnp.max(most, axis=1, keepdims=True) + 1e-06)
    stride = jnp.broadcast_to(stride, (groups, LANES))
    drain_sums(0)
    settle(back_in, back_send.at[0])
    settle(back_in, back_recv.at[0])
    for d in range(3):
        flow = back_out[0, d]
        for offset in range(1, line):
            flow = flow + back_in[offset - 1, d]
        moved = pay_ref[d] + stride * (1.5 * flow - 0.5 * old_ref[d])
        for g in range(groups):
            flow_ref[d : d + 1, g * LANES : (g + 1) * LANES] = flow[g : g + 1]
            moved_ref[d : d + 1, g * LANES : (g + 1) * LANES] = moved[g : g + 1]

    drain_sums(1)
    total = jnp.sum(close_sums(1, len(teams) - 1), axis=1, keepdims=True)
    power_ref[...] = jnp.broadcast_to(
        total * (1.0 / (float(NODES * LANES) * sizes[0] * sizes[1] * sizes[2])), (8, LANES)
    )


def write_out(*refs):
    count = (len(refs) - 2) // 2
    sources, targets = refs[:count], refs[count : 2 * count]
    held, given = refs[2 * count :]
    outward = [pltpu.make_async_copy(sources[i], targets[i], given.at[i]) for i in range(1, count)]
    outward.append(pltpu.make_async_copy(held, targets[0], given.at[0]))
    for copy in outward[:-1]:
        copy.start()
    held[0, 0] = sources[0][0, 0]
    outward[-1].start()
    for copy in outward:
        copy.wait()


def per_device(
    sizes,
    element_ops,
    load_terms,
    trial_velocity,
    tracer_coords,
    tracer_old_velocity,
    host_line,
    host_element_index,
):
    count = host_element_index.shape[0]
    groups = count // LANES
    line = sizes[0]
    direct = max(sizes) <= SWEEPS
    seats = sizes[0] * sizes[1] * sizes[2] if direct else sizes[0] + sizes[1] * sizes[2]
    matrix = jnp.asarray(gradient_matrix()).reshape(3, FINE, 4 * NODES)
    f32 = jnp.float32
    i32 = jnp.int32
    bf16 = jnp.bfloat16
    hbm = pl.BlockSpec(memory_space=pltpu.HBM)
    vmem = pl.BlockSpec(memory_space=pltpu.VMEM)
    dma = pltpu.SemaphoreType.DMA
    small = [pltpu.VMEM((NODES, LANES), f32)] * 4
    operands = (
        element_ops,
        load_terms,
        trial_velocity,
        matrix,
        jnp.asarray(weight_table()),
        tracer_coords,
        tracer_old_velocity,
        host_line.reshape(groups, LANES),
        host_element_index.reshape(groups, LANES),
    )
    solution, velocity, power, flows, moved = pl.pallas_call(
        functools.partial(kernel, sizes, direct),
        out_shape=(
            pltpu.VMEM((NODES, LANES), f32),
            pltpu.VMEM((3, FINE, LANES), bf16),
            pltpu.VMEM((8, LANES), f32),
            pltpu.VMEM((3, count), f32),
            pltpu.VMEM((3, count), f32),
        ),
        in_specs=[hbm] * 9,
        out_specs=(vmem,) * 5,
        scratch_shapes=[
            pltpu.VMEM((NODES, NODES, LANES), f32),
            pltpu.VMEM((NODES, LANES), f32),
            pltpu.VMEM((3, FINE, LANES), f32),
            pltpu.VMEM((3, FINE, 4 * NODES), bf16),
            pltpu.VMEM((8, 8, LANES), f32),
            pltpu.VMEM((3, count), f32),
            pltpu.VMEM((3, count), f32),
            pltpu.VMEM((groups, LANES), i32),
            pltpu.VMEM((groups, LANES), i32),
            pltpu.VMEM((4, groups, LANES), f32),
            pltpu.VMEM((3, groups, LANES), f32),
            *small,
            pltpu.VMEM((4, 40, LANES), f32),
            pltpu.VMEM((3 * NODES, 8 * LANES), bf16),
            pltpu.VMEM((NODES // 8, 8, 8, LANES), f32),
            pltpu.VMEM((SWEEPS + 1, 27, 2 * FACE, LANES), f32),
            pltpu.VMEM((SWEEPS + 1, 27, 2 * FACE, LANES), f32),
            pltpu.VMEM((line - 1, 4, groups, LANES), f32),
            pltpu.VMEM((line, 3, groups, LANES), f32),
            pltpu.VMEM((line - 1, 3, groups, LANES), f32),
            pltpu.VMEM((2, 2, 8, LANES), f32),
            pltpu.VMEM((2, seats, 8, LANES), f32),
            dma((10,)),
            dma((2, 27)),
            dma((2, 27)),
            dma((1,)),
            dma((line - 1,)),
            dma((1,)),
            dma((1,)),
            dma((2, 1 if direct else 2)),
            dma((2, 1 if direct else 2)),
        ],
        compiler_params=pltpu.CompilerParams(
            collective_id=0, has_side_effects=True, vmem_limit_bytes=BRICK_VMEM
        ),
        name="brick",
    )(*(pltpu.with_memory_space_constraint(operand, pltpu.HBM) for operand in operands))
    results = (power, solution, velocity, flows, moved)
    shapes = ((1, 1),) + tuple(r.shape for r in results[1:])
    power, solution, velocity, flows, moved = pl.pallas_call(
        write_out,
        out_shape=tuple(jax.ShapeDtypeStruct(z, r.dtype) for z, r in zip(shapes, results)),
        in_specs=[vmem] + [pl.BlockSpec(memory_space=pl.ANY)] * 4,
        out_specs=(hbm,) * 5,
        scratch_shapes=[pltpu.SMEM((1, 1), f32), dma((5,))],
        compiler_params=pltpu.CompilerParams(vmem_limit_bytes=OUT_VMEM),
        name="write_out",
    )(*results)
    return (solution, velocity, power.reshape(()), flows, moved)


def solution(mesh):
    sizes = tuple(mesh.shape[axis] for axis in AXES)
    placed = (
        P(None, None, AXES),
        P(None, AXES),
        P(None, None, AXES),
        P(None, AXES),
        P(None, AXES),
        P(AXES, None),
        P(AXES),
    )
    return jax.shard_map(
        functools.partial(per_device, sizes),
        mesh=mesh,
        in_specs=placed,
        out_specs=(
            P(None, AXES),
            P(None, None, AXES),
            P(),
            P(None, AXES),
            P(None, AXES),
        ),
        check_vma=False,
    )
```

```python
import functools
import itertools
import math

import jax
import jax.numpy as jnp
import numpy as np
from jax import lax
from jax.experimental import pallas as pl
from jax.experimental.pallas import tpu as pltpu
from jax.sharding import PartitionSpec as P

EX = 4
EY = 4
EZ = 8
SWEEPS = 4
NODES = 64
FACE = 16
LANES = 128
FINE = 512

lower_bound = 0.25
upper_bound = 2.0
courant = 0.5
AXES = ("gx", "gy", "gz")
COUNTS = (EX, EY, EZ)
STEPS = (EY * EZ, EZ, 1)
MESH = pl.DeviceIdType.MESH
FINISH = 3
UNROLL = 4
PAY_SWEEP = 1
SPLIT = 8
BRICK_VMEM = 24 * 1024 * 1024
OUT_VMEM = 4 * 1024 * 1024


def node_tables():
    coarse = -np.cos(np.pi * np.arange(4) / 3.0)
    fine = -np.cos(np.pi * np.arange(8) / 7.0)
    plain = np.zeros((8, 4))
    slope = np.zeros((8, 4))
    for target in range(8):
        for source in range(4):
            others = [other for other in range(4) if other != source]
            value = 1.0
            for other in others:
                value *= (fine[target] - coarse[other]) / (coarse[source] - coarse[other])
            plain[target, source] = value
            total = 0.0
            for skipped in others:
                term = 1.0 / (coarse[source] - coarse[skipped])
                for other in others:
                    if other != skipped:
                        term *= (fine[target] - coarse[other]) / (coarse[source] - coarse[other])
                total += term
            slope[target, source] = total
    return plain, slope, fine


def gradient_matrix():
    plain, slope, _ = node_tables()
    rows = [
        np.kron(np.kron(slope, plain), plain),
        np.kron(np.kron(plain, slope), plain),
        np.kron(np.kron(plain, plain), slope),
    ]
    full = np.concatenate(rows, axis=0).astype(np.float32)
    high = full.astype(jnp.bfloat16)
    low = (full - high.astype(np.float32)).astype(jnp.bfloat16)
    return np.concatenate([high, high, low, high], axis=1)


def weight_table():
    fine = node_tables()[2]
    table = np.zeros((8, 8, LANES), np.float32)
    for target in range(8):
        others = [other for other in range(8) if other != target]
        scale = 1.0
        for j, other in enumerate(others):
            table[j, target] = fine[other]
            scale /= fine[target] - fine[other]
        table[7, target] = scale
    return table


DIRS = [
    (i, j, k)
    for size in (3, 2, 1)
    for i in (-1, 0, 1)
    for j in (-1, 0, 1)
    for k in (-1, 0, 1)
    if abs(i) + abs(j) + abs(k) == size
]


def slot_of(way):
    return (way[0] + 1) * 9 + (way[1] + 1) * 3 + way[2] + 1


def face_rows(way):
    x, y, z = (None if w == 0 else (3 if w > 0 else 0) for w in way)
    if x is not None and y is not None and z is not None:
        return [(16 * x + 4 * y + z, 1, 1)]
    if x is not None and y is not None:
        return [(16 * x + 4 * y, 4, 1)]
    if x is not None and z is not None:
        return [(16 * x + z, 4, 4)]
    if y is not None and z is not None:
        return [(4 * y + z, 4, 16)]
    if x is not None:
        return [(16 * x, 16, 1)]
    if y is not None:
        return [(16 * a + 4 * y, 4, 1) for a in range(4)]
    return [(z, 16, 4)]


def length_of(way):
    return sum(size for _, size, _ in face_rows(way))


def rows_of(piece):
    start, size, stride = piece
    return (pl.ds(start, size, stride=stride) if stride > 1 else pl.ds(start, size), slice(None))


def bit_moves(size):
    return [1 << bit for bit in range(size.bit_length()) if 1 << bit < size]


def kernel(
    sizes,
    direct,
    ops_hbm,
    load_hbm,
    trial_hbm,
    grad_hbm,
    table_hbm,
    coords_hbm,
    old_hbm,
    line_hbm,
    index_hbm,
    sol_ref,
    vel,
    power_ref,
    flow_ref,
    moved_ref,
    ops,
    load,
    trial,
    grad,
    table_ref,
    coords,
    old,
    host,
    index,
    pay_ref,
    old_ref,
    upd,
    res,
    wgt,
    img,
    work,
    wide,
    diag,
    bulk,
    face_out,
    face_in,
    pay_in,
    back_out,
    back_in,
    red_out,
    red_in,
    local_sem,
    face_send,
    face_recv,
    pay_send,
    pay_recv,
    back_send,
    back_recv,
    red_send,
    red_recv,
):
    pairs = [
        (ops_hbm, ops),
        (load_hbm, load),
        (line_hbm, host),
        (index_hbm, index),
        (coords_hbm, coords),
        (old_hbm, old),
        (table_hbm, table_ref),
        (trial_hbm, trial),
        (grad_hbm, grad),
    ]
    loads = [
        pltpu.make_async_copy(src, dst, local_sem.at[i]) for i, (src, dst) in enumerate(pairs)
    ]
    corners = [
        pltpu.make_async_copy(
            ops_hbm.at[pl.ds(n, 8), pl.ds(n, 8)], diag.at[n // 8], local_sem.at[9]
        )
        for n in range(0, NODES, 8)
    ]
    loads[1].start()
    for copy in corners:
        copy.start()
    loads[0].start()

    me = [lax.axis_index(axis) for axis in AXES]
    line = sizes[0]
    groups = pay_ref.shape[1]

    def edge(d, step):
        return me[d] < sizes[d] - 1 if step > 0 else me[d] > 0

    def exists(way):
        tests = [edge(d, way[d]) for d in range(3) if way[d] != 0]
        return functools.reduce(jnp.logical_and, tests)

    present = {way: exists(way) for way in DIRS}

    def beside(way):
        return {AXES[d]: me[d] + way[d] for d in range(3) if way[d] != 0}

    def along(offset):
        there = me[0]
        for bit in bit_moves(line):
            if offset & bit:
                there = there + bit * (1 - 2 * lax.rem(me[0] // bit, 2))
        return {AXES[0]: there}

    def shifted(offset):
        return {
            AXES[d]: lax.rem(me[d] + offset[d], sizes[d]) for d in range(3) if offset[d] != 0
        }

    spans = [range(size) for size in sizes]
    if direct:
        teams = [[(i, j, k) for i in spans[0] for j in spans[1] for k in spans[2]]]
        seats = [(me[0] * sizes[1] + me[1]) * sizes[2] + me[2]]
    else:
        teams = [[(0, j, k) for j in spans[1] for k in spans[2]], [(i, 0, 0) for i in spans[0]]]
        seats = [me[1] * sizes[2] + me[2], me[0]]
    bases = [sum(len(team) for team in teams[:t]) for t in range(len(teams))]

    barrier = pltpu.get_barrier_semaphore()
    held = [
        {w: jnp.clip(me[d] + w, 0, sizes[d] - 1) for w in (-1, 0, 1)} for d in range(3)
    ]
    for way in DIRS:
        near = {AXES[d]: held[d][way[d]] for d in range(3) if way[d] != 0}
        pl.semaphore_signal(barrier, inc=1, device_id=near, device_id_type=MESH)

    partners = [along(offset) for offset in range(1, line)]
    if not direct:
        partners += [shifted(offset) for team in teams for offset in team[1:]]
    for partner in partners:
        pl.semaphore_signal(barrier, inc=1, device_id=partner, device_id_type=MESH)

    for copy in loads[2:7]:
        copy.start()

    for way in DIRS:

        @pl.when(jnp.logical_not(present[way]))
        def _():
            for x in range(SWEEPS + 1):
                face_in[x, slot_of(way)] = jnp.zeros((2 * FACE, LANES), jnp.float32)

    lane = lax.broadcasted_iota(jnp.int32, (40, LANES), 1)
    place = [lane // (EY * EZ), lane // EZ % EY, lane % EZ]

    def parts_of(x):
        return 2 if x == 0 else 1

    def face_copy(x, way):
        rows = parts_of(x) * length_of(way)
        there = slot_of(tuple(-w for w in way))
        return pltpu.make_async_remote_copy(
            src_ref=face_out.at[x, slot_of(way), pl.ds(0, rows)],
            dst_ref=face_in.at[x, there, pl.ds(0, rows)],
            send_sem=face_send.at[x % 2],
            recv_sem=face_recv.at[x % 2],
            device_id=beside(way),
            device_id_type=MESH,
        )

    def fill_faces(x, parts, ways):
        for way in ways:
            at = 0
            for ref in parts:
                for piece in face_rows(way):
                    face_out[x, slot_of(way), at : at + piece[1]] = ref[rows_of(piece)]
                    at += piece[1]

    def start_faces(x, ways):
        for way in ways:

            @pl.when(present[way])
            def _():
                face_copy(x, way).start()

    def settle(view, sem):
        pltpu.make_async_copy(view, view, sem).wait()

    between = [jnp.logical_and(edge(d, -1), edge(d, 1)) for d in range(3)]

    def settle_faces(x, sem):
        for near in itertools.product(*[(min(size - 1, 1), 2)[: min(size - 1, 2)] for size in sizes]):
            rows = sum(
                length_of(way) * math.prod(near[d] for d in range(3) if way[d])
                for way in itertools.product((0, 1), repeat=3)
                if any(way)
            )
            tests = [
                between[d] if near[d] == 2 else jnp.logical_not(between[d])
                for d in range(3)
                if sizes[d] > 2
            ]

            @pl.when(functools.reduce(jnp.logical_and, tests))
            def _():
                settle(bulk.at[pl.ds(0, parts_of(x) * rows)], sem)

    def drain_faces(x):
        settle_faces(x, face_send.at[x % 2])

    def open_faces(x, parts):
        for group in (DIRS[:8], DIRS[8:20], DIRS[20:]):
            fill_faces(x, parts, group)
            start_faces(x, group)

    def combine(d, pieces):
        at = 0
        for size, *places in pieces:
            for s, (ref, piece) in enumerate(places):
                work[s, at : at + size] = ref[rows_of(piece)]
            at += size
        count, step = COUNTS[d], STEPS[d]
        far = (count - 1) * step
        total = -(-at // 8) * 8
        low, high, before, after = (work[s, 0:total] for s in range(4))
        where_at = place[d][0:total]
        new = (
            low
            + jnp.where(
                where_at > 0,
                pltpu.roll(high, step, 1),
                pltpu.roll(before, (LANES - far) % LANES, 1),
            ),
            high
            + jnp.where(
                where_at < count - 1,
                pltpu.roll(low, LANES - step, 1),
                pltpu.roll(after, far, 1),
            ),
        )
        at = 0
        for size, *places in pieces:
            for s in range(2):
                ref, piece = places[s]
                ref[rows_of(piece)] = new[s][at : at + size]
            at += size

    def close_faces(x, parts):
        settle_faces(x, face_recv.at[x % 2])

        ends = (-1, 1)
        for p, ref in enumerate(parts):

            def got(way, start=0, size=None, stride=1):
                full = length_of(way)
                return (
                    face_in.at[x, slot_of(way)],
                    (p * full + start, full if size is None else size, stride),
                )

            pieces = [(16, (ref, (0, 16, 1)), (ref, (48, 16, 1)), got((-1, 0, 0)), got((1, 0, 0)))]
            for o in ends:
                for way in ((0, o, 0), (0, 0, o)):
                    lo, hi = (-1, *way[1:]), (1, *way[1:])
                    pieces.append((4, got(way, 0, 4), got(way, 12, 4), got(lo), got(hi)))
            for oy in ends:
                for oz in ends:
                    way = (0, oy, oz)
                    pieces.append(
                        (1, got(way, 0, 1), got(way, 3, 1), got((-1, oy, oz)), got((1, oy, oz)))
                    )
            combine(0, pieces)
            pieces = []
            for a in range(4):
                pieces.append(
                    (
                        4,
                        (ref, (16 * a, 4, 1)),
                        (ref, (16 * a + 12, 4, 1)),
                        got((0, -1, 0), 4 * a, 4),
                        got((0, 1, 0), 4 * a, 4),
                    )
                )
            for oz in ends:
                way = (0, 0, oz)
                pieces.append(
                    (4, got(way, 0, 4, 4), got(way, 3, 4, 4), got((0, -1, oz)), got((0, 1, oz)))
                )
            combine(1, pieces)
            combine(
                2,
                [(16, (ref, (0, 16, 4)), (ref, (3, 16, 4)), got((0, 0, -1)), got((0, 0, 1)))],
            )

    def apply_operator():
        def block(i, total):
            rows = upd[pl.ds(pl.multiple_of(8 * i, 8), 8), :]
            for j in range(8):
                total = total + ops[8 * i + j] * rows[j : j + 1, :]
            return total

        img[...] = lax.fori_loop(0, NODES // 8, block, jnp.zeros((NODES, LANES), jnp.float32), unroll=SPLIT)

    def pay_copy(offset):
        return pltpu.make_async_remote_copy(
            src_ref=pay_ref,
            dst_ref=pay_in.at[offset - 1],
            send_sem=pay_send.at[0],
            recv_sem=pay_recv.at[offset - 1],
            device_id=along(offset),
            device_id_type=MESH,
        )

    def back_copy(offset):
        return pltpu.make_async_remote_copy(
            src_ref=back_out.at[offset],
            dst_ref=back_in.at[offset - 1],
            send_sem=back_send.at[0],
            recv_sem=back_recv.at[0],
            device_id=along(offset),
            device_id_type=MESH,
        )

    def red_copy(kind, t, offset):
        return pltpu.make_async_remote_copy(
            src_ref=red_out.at[kind, t, pl.ds(0, 1)],
            dst_ref=red_in.at[kind, bases[t] + seats[t], pl.ds(0, 1)],
            send_sem=red_send.at[kind, t],
            recv_sem=red_recv.at[kind, t],
            device_id=shifted(teams[t][offset]),
            device_id_type=MESH,
        )

    def others(kind, t):
        return red_in.at[kind, pl.ds(bases[t], len(teams[t]) - 1), pl.ds(0, 1)]

    def open_sums(kind, t, value):
        red_out[kind, t, 0:1] = value
        for offset in range(len(teams[t]) - 1, 0, -1):
            red_copy(kind, t, offset).start()
        red_in[kind, bases[t] + seats[t], 0:1] = value

    def close_sums(kind, t):
        settle(others(kind, t), red_recv.at[kind, t])
        values = [red_in[kind, bases[t] + i, 0:1] for i in range(len(teams[t]))]
        join = jnp.add if kind else jnp.maximum
        while len(values) > 1:
            values = [
                join(*values[i : i + 2]) if i + 1 < len(values) else values[i]
                for i in range(0, len(values), 2)
            ]
        return values[0]

    def drain_sums(kind):
        for t in range(len(teams)):
            settle(others(kind, t), red_send.at[kind, t])

    loads[1].wait()
    settle(ops.at[pl.ds(0, 8)], local_sem.at[9])
    res[...] = load[...]
    for n in range(NODES):
        wgt[n : n + 1, :] = diag[n // 8, n % 8, n % 8 : n % 8 + 1, :]
    fill_faces(0, (res, wgt), DIRS)
    pl.semaphore_wait(barrier, len(partners) + len(DIRS))

    start_faces(0, DIRS)
    for copy in loads[2:7]:
        copy.wait()
    pay_ref[3] = (host[...] * LANES + index[...]).astype(jnp.float32)
    for d in range(3):
        for g in range(groups):
            lanes = slice(g * LANES, (g + 1) * LANES)
            pay_ref[d, g : g + 1, :] = coords[d : d + 1, lanes]
            old_ref[d, g : g + 1, :] = old[d : d + 1, lanes]
    order = range(line - 1, 0, -1)
    for copy in loads[7:]:
        copy.start()
    close_faces(0, (res, wgt))

    loads[0].wait()
    center = 0.5 * (upper_bound + lower_bound)
    radius = 0.5 * (upper_bound - lower_bound)
    sigma = center / radius
    rho = 1.0 / sigma
    upd[...] = res[...] / (center * wgt[...])
    sol_ref[...] = upd[...]
    for sweep in range(SWEEPS - 1):
        apply_operator()
        open_faces(sweep + 1, (img,))
        if sweep == PAY_SWEEP:
            for offset in order:
                pay_copy(offset).start()
        drain_faces(sweep)
        if sweep + 2 == SWEEPS:
            for copy in loads[7:]:
                copy.wait()
            settle(pay_in, pay_send.at[0])
        close_faces(sweep + 1, (img,))
        left = res[...] - img[...]
        res[...] = left
        rho_next = 1.0 / (2.0 * sigma - rho)
        new = (rho_next * rho) * upd[...] + (2.0 * rho_next / radius) * left / wgt[...]
        rho = rho_next
        upd[...] = new
        sol_ref[...] = sol_ref[...] + new

    last = SWEEPS
    apply_operator()
    open_faces(last, (img,))

    pressure = sol_ref[...]
    p_high = pressure.astype(jnp.bfloat16)
    rest = pressure - p_high.astype(jnp.float32)
    p_mid = rest.astype(jnp.bfloat16)
    p_low = (rest - p_mid.astype(jnp.float32)).astype(jnp.bfloat16)
    pieces = jnp.concatenate([p_high, p_mid, p_high, p_low], axis=0)
    speed = jnp.zeros((FINE, LANES), jnp.float32)
    for d in range(3):
        slope = jnp.dot(grad[d], pieces, preferred_element_type=jnp.float32)
        value = (trial[d] - slope).astype(jnp.bfloat16)
        vel[d] = value
        for k in range(8):
            wide[64 * d : 64 * d + 64, LANES * k : LANES * (k + 1)] = value[64 * k : 64 * k + 64]
        speed = speed + jnp.abs(value.astype(jnp.float32))
    open_sums(0, 0, jnp.max(speed, axis=0, keepdims=True))

    element = lax.broadcasted_iota(jnp.int32, (LANES, LANES), 0).astype(jnp.float32)
    own_first = (me[0] * LANES).astype(jnp.float32)

    def interpolate(source, target, first, end):
        def lagrange(point):
            value = table_ref[7]
            for j in range(7):
                value = value * (point - table_ref[j])
            return value

        def spread(row):
            row = jnp.broadcast_to(row, (16, LANES)).astype(jnp.bfloat16)
            return jnp.concatenate([row] * (LANES // 16), axis=0)

        def one_tile(i, carry):
            chosen = []
            weights = []
            for h in range(2):
                row = pl.ds(2 * i + h, 1)
                key = source[3, row, :] - own_first
                hot = jnp.where(element == key, 1.0, 0.0).astype(jnp.bfloat16)
                w_x, w_y, w_z = (lagrange(source[axis, row, :]) for axis in range(3))
                weights.append((w_y, w_z))
                chosen.append(
                    jnp.concatenate([hot * spread(w_x[k : k + 1]) for k in range(8)], axis=0)
                )
            taken = jnp.dot(
                wide[...],
                jnp.concatenate(chosen, axis=1),
                preferred_element_type=jnp.float32,
            )
            for d in range(3):
                for h in range(2):
                    part = taken[64 * d : 64 * d + 64, h * LANES : (h + 1) * LANES]
                    w_y, w_z = weights[h]
                    over_y = w_y[0:1] * part[0:8]
                    for l in range(1, 8):
                        over_y = over_y + w_y[l : l + 1] * part[8 * l : 8 * l + 8]
                    target[d, pl.ds(2 * i + h, 1), :] = jnp.sum(
                        w_z * over_y, axis=0, keepdims=True
                    )
            return carry

        lax.fori_loop(first, end, one_tile, 0, unroll=UNROLL)

    def finish_faces():
        drain_faces(last - 1)
        close_faces(last, (img,))
        left = res[...] - img[...]
        open_sums(1, 0, jnp.sum(left * left, axis=0, keepdims=True))

    tiles = groups // 2
    half = tiles // 2
    turn = 0
    for offset in order:
        pay_copy(offset).wait_recv()
        for first, end in ((0, half), (half, tiles)):
            interpolate(pay_in.at[offset - 1], back_out.at[offset], first, end)
            if end == tiles:
                back_copy(offset).start()
            turn += 1
            if turn == FINISH:
                finish_faces()
    if turn < FINISH:
        finish_faces()
    interpolate(pay_ref, back_out.at[0], 0, tiles)

    drain_faces(last)
    most = close_sums(0, 0)
    for t in range(1, len(teams)):
        open_sums(0, t, most)
        open_sums(1, t, close_sums(1, t - 1))
        most = close_sums(0, t)
    stride = courant / (jnp.max(most, axis=1, keepdims=True) + 1e-06)
    stride = jnp.broadcast_to(stride, (groups, LANES))
    drain_sums(0)
    settle(back_in, back_send.at[0])
    settle(back_in, back_recv.at[0])
    for d in range(3):
        flow = back_out[0, d]
        for offset in range(1, line):
            flow = flow + back_in[offset - 1, d]
        moved = pay_ref[d] + stride * (1.5 * flow - 0.5 * old_ref[d])
        for g in range(groups):
            flow_ref[d : d + 1, g * LANES : (g + 1) * LANES] = flow[g : g + 1]
            moved_ref[d : d + 1, g * LANES : (g + 1) * LANES] = moved[g : g + 1]

    drain_sums(1)
    total = jnp.sum(close_sums(1, len(teams) - 1), axis=1, keepdims=True)
    power_ref[...] = jnp.broadcast_to(
        total * (1.0 / (float(NODES * LANES) * sizes[0] * sizes[1] * sizes[2])), (8, LANES)
    )


def write_out(*refs):
    count = (len(refs) - 2) // 2
    sources, targets = refs[:count], refs[count : 2 * count]
    held, given = refs[2 * count :]
    outward = [pltpu.make_async_copy(sources[i], targets[i], given.at[i]) for i in range(1, count)]
    outward.append(pltpu.make_async_copy(held, targets[0], given.at[0]))
    for copy in outward[:-1]:
        copy.start()
    held[0, 0] = sources[0][0, 0]
    outward[-1].start()
    for copy in outward:
        copy.wait()


def per_device(
    sizes,
    element_ops,
    load_terms,
    trial_velocity,
    tracer_coords,
    tracer_old_velocity,
    host_line,
    host_element_index,
):
    count = host_element_index.shape[0]
    groups = count // LANES
    line = sizes[0]
    direct = max(sizes) <= SWEEPS
    seats = sizes[0] * sizes[1] * sizes[2] if direct else sizes[0] + sizes[1] * sizes[2]
    matrix = jnp.asarray(gradient_matrix()).reshape(3, FINE, 4 * NODES)
    f32 = jnp.float32
    i32 = jnp.int32
    bf16 = jnp.bfloat16
    hbm = pl.BlockSpec(memory_space=pltpu.HBM)
    vmem = pl.BlockSpec(memory_space=pltpu.VMEM)
    dma = pltpu.SemaphoreType.DMA
    small = [pltpu.VMEM((NODES, LANES), f32)] * 4
    operands = (
        element_ops,
        load_terms,
        trial_velocity,
        matrix,
        jnp.asarray(weight_table()),
        tracer_coords,
        tracer_old_velocity,
        host_line.reshape(groups, LANES),
        host_element_index.reshape(groups, LANES),
    )
    solution, velocity, power, flows, moved = pl.pallas_call(
        functools.partial(kernel, sizes, direct),
        out_shape=(
            pltpu.VMEM((NODES, LANES), f32),
            pltpu.VMEM((3, FINE, LANES), bf16),
            pltpu.VMEM((8, LANES), f32),
            pltpu.VMEM((3, count), f32),
            pltpu.VMEM((3, count), f32),
        ),
        in_specs=[hbm] * 9,
        out_specs=(vmem,) * 5,
        scratch_shapes=[
            pltpu.VMEM((NODES, NODES, LANES), f32),
            pltpu.VMEM((NODES, LANES), f32),
            pltpu.VMEM((3, FINE, LANES), f32),
            pltpu.VMEM((3, FINE, 4 * NODES), bf16),
            pltpu.VMEM((8, 8, LANES), f32),
            pltpu.VMEM((3, count), f32),
            pltpu.VMEM((3, count), f32),
            pltpu.VMEM((groups, LANES), i32),
            pltpu.VMEM((groups, LANES), i32),
            pltpu.VMEM((4, groups, LANES), f32),
            pltpu.VMEM((3, groups, LANES), f32),
            *small,
            pltpu.VMEM((4, 40, LANES), f32),
            pltpu.VMEM((3 * NODES, 8 * LANES), bf16),
            pltpu.VMEM((NODES // 8, 8, 8, LANES), f32),
            pltpu.VMEM((20 * FACE, LANES), f32),
            pltpu.VMEM((SWEEPS + 1, 27, 2 * FACE, LANES), f32),
            pltpu.VMEM((SWEEPS + 1, 27, 2 * FACE, LANES), f32),
            pltpu.VMEM((line - 1, 4, groups, LANES), f32),
            pltpu.VMEM((line, 3, groups, LANES), f32),
            pltpu.VMEM((line - 1, 3, groups, LANES), f32),
            pltpu.VMEM((2, 2, 8, LANES), f32),
            pltpu.VMEM((2, seats, 8, LANES), f32),
            dma((10,)),
            dma((2,)),
            dma((2,)),
            dma((1,)),
            dma((line - 1,)),
            dma((1,)),
            dma((1,)),
            dma((2, 1 if direct else 2)),
            dma((2, 1 if direct else 2)),
        ],
        compiler_params=pltpu.CompilerParams(
            collective_id=0, has_side_effects=True, vmem_limit_bytes=BRICK_VMEM
        ),
        name="brick",
    )(*(pltpu.with_memory_space_constraint(operand, pltpu.HBM) for operand in operands))
    results = (power, solution, velocity, flows, moved)
    shapes = ((1, 1),) + tuple(r.shape for r in results[1:])
    power, solution, velocity, flows, moved = pl.pallas_call(
        write_out,
        out_shape=tuple(jax.ShapeDtypeStruct(z, r.dtype) for z, r in zip(shapes, results)),
        in_specs=[vmem] + [pl.BlockSpec(memory_space=pl.ANY)] * 4,
        out_specs=(hbm,) * 5,
        scratch_shapes=[pltpu.SMEM((1, 1), f32), dma((5,))],
        compiler_params=pltpu.CompilerParams(vmem_limit_bytes=OUT_VMEM),
        name="write_out",
    )(*results)
    return (solution, velocity, power.reshape(()), flows, moved)


def solution(mesh):
    sizes = tuple(mesh.shape[axis] for axis in AXES)
    placed = (
        P(None, None, AXES),
        P(None, AXES),
        P(None, None, AXES),
        P(None, AXES),
        P(None, AXES),
        P(AXES, None),
        P(AXES),
    )
    return jax.shard_map(
        functools.partial(per_device, sizes),
        mesh=mesh,
        in_specs=placed,
        out_specs=(
            P(None, AXES),
            P(None, None, AXES),
            P(),
            P(None, AXES),
            P(None, AXES),
        ),
        check_vma=False,
    )
```

```python
import functools
import itertools
import math

import jax
import jax.numpy as jnp
import numpy as np
from jax import lax
from jax.experimental import pallas as pl
from jax.experimental.pallas import tpu as pltpu
from jax.sharding import PartitionSpec as P

EX = 4
EY = 4
EZ = 8
SWEEPS = 4
NODES = 64
FACE = 16
LANES = 128
FINE = 512

lower_bound = 0.25
upper_bound = 2.0
courant = 0.5
AXES = ("gx", "gy", "gz")
COUNTS = (EX, EY, EZ)
STEPS = (EY * EZ, EZ, 1)
MESH = pl.DeviceIdType.MESH
FINISH = 3
UNROLL = 4
SPLIT = 8
BRICK_VMEM = 24 * 1024 * 1024
OUT_VMEM = 4 * 1024 * 1024


def node_tables():
    coarse = -np.cos(np.pi * np.arange(4) / 3.0)
    fine = -np.cos(np.pi * np.arange(8) / 7.0)
    plain = np.zeros((8, 4))
    slope = np.zeros((8, 4))
    for target in range(8):
        for source in range(4):
            others = [other for other in range(4) if other != source]
            value = 1.0
            for other in others:
                value *= (fine[target] - coarse[other]) / (coarse[source] - coarse[other])
            plain[target, source] = value
            total = 0.0
            for skipped in others:
                term = 1.0 / (coarse[source] - coarse[skipped])
                for other in others:
                    if other != skipped:
                        term *= (fine[target] - coarse[other]) / (coarse[source] - coarse[other])
                total += term
            slope[target, source] = total
    return plain, slope, fine


def gradient_matrix():
    plain, slope, _ = node_tables()
    rows = [
        np.kron(np.kron(slope, plain), plain),
        np.kron(np.kron(plain, slope), plain),
        np.kron(np.kron(plain, plain), slope),
    ]
    full = np.concatenate(rows, axis=0).astype(np.float32)
    high = full.astype(jnp.bfloat16)
    low = (full - high.astype(np.float32)).astype(jnp.bfloat16)
    return np.concatenate([high, high, low, high], axis=1)


def weight_table():
    fine = node_tables()[2]
    table = np.zeros((8, 8, LANES), np.float32)
    for target in range(8):
        others = [other for other in range(8) if other != target]
        scale = 1.0
        for j, other in enumerate(others):
            table[j, target] = fine[other]
            scale /= fine[target] - fine[other]
        table[7, target] = scale
    return table


def rank(way):
    size = sum(abs(w) for w in way)
    return -1 if size == 2 and way[1] == 0 else 3 - size


DIRS = sorted(
    ((i, j, k) for i in (-1, 0, 1) for j in (-1, 0, 1) for k in (-1, 0, 1) if i or j or k),
    key=rank,
)


def slot_of(way):
    return (way[0] + 1) * 9 + (way[1] + 1) * 3 + way[2] + 1


def face_rows(way):
    x, y, z = (None if w == 0 else (3 if w > 0 else 0) for w in way)
    if x is not None and y is not None and z is not None:
        return [(16 * x + 4 * y + z, 1, 1)]
    if x is not None and y is not None:
        return [(16 * x + 4 * y, 4, 1)]
    if x is not None and z is not None:
        return [(16 * x + z, 4, 4)]
    if y is not None and z is not None:
        return [(4 * y + z, 4, 16)]
    if x is not None:
        return [(16 * x, 16, 1)]
    if y is not None:
        return [(16 * a + 4 * y, 4, 1) for a in range(4)]
    return [(z, 16, 4)]


def length_of(way):
    return sum(size for _, size, _ in face_rows(way))


def rows_of(piece):
    start, size, stride = piece
    return (pl.ds(start, size, stride=stride) if stride > 1 else pl.ds(start, size), slice(None))


def bit_moves(size):
    return [1 << bit for bit in range(size.bit_length()) if 1 << bit < size]


def kernel(
    sizes,
    direct,
    ops_hbm,
    load_hbm,
    trial_hbm,
    grad_hbm,
    table_hbm,
    coords_hbm,
    old_hbm,
    line_hbm,
    index_hbm,
    sol_ref,
    vel,
    power_ref,
    flow_ref,
    moved_ref,
    ops,
    load,
    trial,
    grad,
    table_ref,
    coords,
    old,
    host,
    index,
    pay_ref,
    old_ref,
    upd,
    res,
    wgt,
    img,
    work,
    wide,
    diag,
    bulk,
    face_out,
    face_in,
    pay_in,
    back_out,
    back_in,
    red_out,
    red_in,
    local_sem,
    face_send,
    face_recv,
    pay_send,
    pay_recv,
    back_send,
    back_recv,
    red_send,
    red_recv,
):
    pairs = [
        (ops_hbm, ops),
        (load_hbm, load),
        (line_hbm, host),
        (index_hbm, index),
        (coords_hbm, coords),
        (old_hbm, old),
        (table_hbm, table_ref),
        (trial_hbm, trial),
        (grad_hbm, grad),
    ]
    loads = [
        pltpu.make_async_copy(src, dst, local_sem.at[i]) for i, (src, dst) in enumerate(pairs)
    ]
    corners = [
        pltpu.make_async_copy(
            ops_hbm.at[pl.ds(n, 8), pl.ds(n, 8)], diag.at[n // 8], local_sem.at[9]
        )
        for n in range(0, NODES, 8)
    ]
    loads[1].start()
    for copy in corners:
        copy.start()
    loads[0].start()

    me = [lax.axis_index(axis) for axis in AXES]
    line = sizes[0]
    groups = pay_ref.shape[1]

    def edge(d, step):
        return me[d] < sizes[d] - 1 if step > 0 else me[d] > 0

    def exists(way):
        tests = [edge(d, way[d]) for d in range(3) if way[d] != 0]
        return functools.reduce(jnp.logical_and, tests)

    present = {way: exists(way) for way in DIRS}

    def beside(way):
        return {AXES[d]: me[d] + way[d] for d in range(3) if way[d] != 0}

    def moved_by(d, offset):
        there = me[d]
        for bit in bit_moves(sizes[d]):
            if offset & bit:
                there = there + bit * (1 - 2 * lax.rem(me[d] // bit, 2))
        return there

    moves = [[moved_by(d, offset) for offset in range(sizes[d])] for d in range(3)]

    def along(offset):
        return {AXES[0]: moves[0][offset]}

    def shifted(offset):
        return {AXES[d]: moves[d][offset[d]] for d in range(3) if offset[d] != 0}

    spans = [range(size) for size in sizes]
    if direct:
        teams = [[(i, j, k) for i in spans[0] for j in spans[1] for k in spans[2]]]
        seats = [(me[0] * sizes[1] + me[1]) * sizes[2] + me[2]]
    else:
        teams = [[(0, j, k) for j in spans[1] for k in spans[2]], [(i, 0, 0) for i in spans[0]]]
        seats = [me[1] * sizes[2] + me[2], me[0]]
    bases = [sum(len(team) for team in teams[:t]) for t in range(len(teams))]

    barrier = pltpu.get_barrier_semaphore()
    held = [
        {w: jnp.clip(me[d] + w, 0, sizes[d] - 1) for w in (-1, 0, 1)} for d in range(3)
    ]
    for way in DIRS:
        near = {AXES[d]: held[d][way[d]] for d in range(3) if way[d] != 0}
        pl.semaphore_signal(barrier, inc=1, device_id=near, device_id_type=MESH)

    partners = [along(offset) for offset in range(1, line)]
    if not direct:
        partners += [shifted(offset) for team in teams for offset in team[1:]]
    for partner in partners:
        pl.semaphore_signal(barrier, inc=1, device_id=partner, device_id_type=MESH)

    for copy in loads[2:7]:
        copy.start()

    lane = lax.broadcasted_iota(jnp.int32, (40, LANES), 1)
    place = [lane // (EY * EZ), lane // EZ % EY, lane % EZ]

    def parts_of(x):
        return 2 if x == 0 else 1

    def clear_faces(rounds):
        for way in DIRS:

            @pl.when(jnp.logical_not(present[way]))
            def _():
                for x in rounds:
                    rows = -(-parts_of(x) * length_of(way) // 8) * 8
                    face_in[x, slot_of(way), 0:rows] = jnp.zeros((rows, LANES), jnp.float32)

    def face_copy(x, way):
        rows = parts_of(x) * length_of(way)
        there = slot_of(tuple(-w for w in way))
        return pltpu.make_async_remote_copy(
            src_ref=face_out.at[x, slot_of(way), pl.ds(0, rows)],
            dst_ref=face_in.at[x, there, pl.ds(0, rows)],
            send_sem=face_send.at[x % 2],
            recv_sem=face_recv.at[x % 2],
            device_id=beside(way),
            device_id_type=MESH,
        )

    def fill_faces(x, parts, ways):
        for way in ways:
            at = 0
            for ref in parts:
                for piece in face_rows(way):
                    face_out[x, slot_of(way), at : at + piece[1]] = ref[rows_of(piece)]
                    at += piece[1]

    def start_faces(x, ways):
        for way in ways:

            @pl.when(present[way])
            def _():
                face_copy(x, way).start()

    def settle(view, sem):
        pltpu.make_async_copy(view, view, sem).wait()

    between = [jnp.logical_and(edge(d, -1), edge(d, 1)) for d in range(3)]

    def settle_faces(x, sem):
        for near in itertools.product(*[(min(size - 1, 1), 2)[: min(size - 1, 2)] for size in sizes]):
            rows = sum(
                length_of(way) * math.prod(near[d] for d in range(3) if way[d])
                for way in itertools.product((0, 1), repeat=3)
                if any(way)
            )
            tests = [
                between[d] if near[d] == 2 else jnp.logical_not(between[d])
                for d in range(3)
                if sizes[d] > 2
            ]

            @pl.when(functools.reduce(jnp.logical_and, tests))
            def _():
                settle(bulk.at[pl.ds(0, parts_of(x) * rows)], sem)

    def drain_faces(x):
        settle_faces(x, face_send.at[x % 2])

    def open_faces(x, parts):
        for group in (DIRS[:12], DIRS[12:20], DIRS[20:]):
            fill_faces(x, parts, group)
            start_faces(x, group)

    def combine(d, pieces):
        at = 0
        for size, *places in pieces:
            for s, (ref, piece) in enumerate(places):
                work[s, at : at + size] = ref[rows_of(piece)]
            at += size
        count, step = COUNTS[d], STEPS[d]
        far = (count - 1) * step
        total = -(-at // 8) * 8
        low, high, before, after = (work[s, 0:total] for s in range(4))
        where_at = place[d][0:total]
        new = (
            low
            + jnp.where(
                where_at > 0,
                pltpu.roll(high, step, 1),
                pltpu.roll(before, (LANES - far) % LANES, 1),
            ),
            high
            + jnp.where(
                where_at < count - 1,
                pltpu.roll(low, LANES - step, 1),
                pltpu.roll(after, far, 1),
            ),
        )
        at = 0
        for size, *places in pieces:
            for s in range(2):
                ref, piece = places[s]
                ref[rows_of(piece)] = new[s][at : at + size]
            at += size

    def close_faces(x, parts):
        settle_faces(x, face_recv.at[x % 2])

        ends = (-1, 1)
        for p, ref in enumerate(parts):

            def got(way, start=0, size=None, stride=1):
                full = length_of(way)
                return (
                    face_in.at[x, slot_of(way)],
                    (p * full + start, full if size is None else size, stride),
                )

            pieces = [(16, (ref, (0, 16, 1)), (ref, (48, 16, 1)), got((-1, 0, 0)), got((1, 0, 0)))]
            for o in ends:
                for way in ((0, o, 0), (0, 0, o)):
                    lo, hi = (-1, *way[1:]), (1, *way[1:])
                    pieces.append((4, got(way, 0, 4), got(way, 12, 4), got(lo), got(hi)))
            for oy in ends:
                for oz in ends:
                    way = (0, oy, oz)
                    pieces.append(
                        (1, got(way, 0, 1), got(way, 3, 1), got((-1, oy, oz)), got((1, oy, oz)))
                    )
            combine(0, pieces)
            pieces = []
            for a in range(4):
                pieces.append(
                    (
                        4,
                        (ref, (16 * a, 4, 1)),
                        (ref, (16 * a + 12, 4, 1)),
                        got((0, -1, 0), 4 * a, 4),
                        got((0, 1, 0), 4 * a, 4),
                    )
                )
            for oz in ends:
                way = (0, 0, oz)
                pieces.append(
                    (4, got(way, 0, 4, 4), got(way, 3, 4, 4), got((0, -1, oz)), got((0, 1, oz)))
                )
            combine(1, pieces)
            combine(
                2,
                [(16, (ref, (0, 16, 4)), (ref, (3, 16, 4)), got((0, 0, -1)), got((0, 0, 1)))],
            )

    def apply_operator():
        def block(i, total):
            rows = upd[pl.ds(pl.multiple_of(8 * i, 8), 8), :]
            for j in range(8):
                total = total + ops[8 * i + j] * rows[j : j + 1, :]
            return total

        img[...] = lax.fori_loop(0, NODES // 8, block, jnp.zeros((NODES, LANES), jnp.float32), unroll=SPLIT)

    def pay_copy(offset):
        return pltpu.make_async_remote_copy(
            src_ref=pay_ref,
            dst_ref=pay_in.at[offset - 1],
            send_sem=pay_send.at[0],
            recv_sem=pay_recv.at[offset - 1],
            device_id=along(offset),
            device_id_type=MESH,
        )

    def back_copy(offset):
        return pltpu.make_async_remote_copy(
            src_ref=back_out.at[offset],
            dst_ref=back_in.at[offset - 1],
            send_sem=back_send.at[0],
            recv_sem=back_recv.at[0],
            device_id=along(offset),
            device_id_type=MESH,
        )

    def red_copy(kind, t, offset):
        return pltpu.make_async_remote_copy(
            src_ref=red_out.at[kind, t, pl.ds(0, 1)],
            dst_ref=red_in.at[kind, bases[t] + seats[t], pl.ds(0, 1)],
            send_sem=red_send.at[kind, t],
            recv_sem=red_recv.at[kind, t],
            device_id=shifted(teams[t][offset]),
            device_id_type=MESH,
        )

    def others(kind, t):
        return red_in.at[kind, pl.ds(bases[t], len(teams[t]) - 1), pl.ds(0, 1)]

    def open_sums(kind, t, value):
        red_out[kind, t, 0:1] = value
        for offset in range(len(teams[t]) - 1, 0, -1):
            red_copy(kind, t, offset).start()
        red_in[kind, bases[t] + seats[t], 0:1] = value

    def close_sums(kind, t):
        settle(others(kind, t), red_recv.at[kind, t])
        values = [red_in[kind, bases[t] + i, 0:1] for i in range(len(teams[t]))]
        join = jnp.add if kind else jnp.maximum
        while len(values) > 1:
            values = [
                join(*values[i : i + 2]) if i + 1 < len(values) else values[i]
                for i in range(0, len(values), 2)
            ]
        return values[0]

    def drain_sums(kind):
        for t in range(len(teams)):
            settle(others(kind, t), red_send.at[kind, t])

    loads[1].wait()
    settle(ops.at[pl.ds(0, 8)], local_sem.at[9])
    res[...] = load[...]
    for n in range(NODES):
        wgt[n : n + 1, :] = diag[n // 8, n % 8, n % 8 : n % 8 + 1, :]
    fill_faces(0, (res, wgt), DIRS)
    pl.semaphore_wait(barrier, len(partners) + len(DIRS))

    start_faces(0, DIRS)
    clear_faces(range(SWEEPS + 1))
    for copy in loads[2:7]:
        copy.wait()
    pay_ref[3] = (host[...] * LANES + index[...]).astype(jnp.float32)
    for d in range(3):
        for g in range(groups):
            lanes = slice(g * LANES, (g + 1) * LANES)
            pay_ref[d, g : g + 1, :] = coords[d : d + 1, lanes]
            old_ref[d, g : g + 1, :] = old[d : d + 1, lanes]
    order = range(line - 1, 0, -1)
    for copy in loads[7:]:
        copy.start()
    close_faces(0, (res, wgt))

    loads[0].wait()
    center = 0.5 * (upper_bound + lower_bound)
    radius = 0.5 * (upper_bound - lower_bound)
    sigma = center / radius
    rho = 1.0 / sigma
    upd[...] = res[...] / (center * wgt[...])
    sol_ref[...] = upd[...]
    for sweep in range(SWEEPS - 1):
        apply_operator()
        open_faces(sweep + 1, (img,))
        for turn, offset in enumerate(order):
            if sweep == min(turn, SWEEPS - 2):
                pay_copy(offset).start()
        drain_faces(sweep)
        if sweep + 2 == SWEEPS:
            for copy in loads[7:]:
                copy.wait()
            settle(pay_in, pay_send.at[0])
        close_faces(sweep + 1, (img,))
        left = res[...] - img[...]
        res[...] = left
        rho_next = 1.0 / (2.0 * sigma - rho)
        new = (rho_next * rho) * upd[...] + (2.0 * rho_next / radius) * left / wgt[...]
        rho = rho_next
        upd[...] = new
        sol_ref[...] = sol_ref[...] + new

    last = SWEEPS
    apply_operator()
    open_faces(last, (img,))

    pressure = sol_ref[...]
    p_high = pressure.astype(jnp.bfloat16)
    rest = pressure - p_high.astype(jnp.float32)
    p_mid = rest.astype(jnp.bfloat16)
    p_low = (rest - p_mid.astype(jnp.float32)).astype(jnp.bfloat16)
    pieces = jnp.concatenate([p_high, p_mid, p_high, p_low], axis=0)
    speed = jnp.zeros((FINE, LANES), jnp.float32)
    for d in range(3):
        slope = jnp.dot(grad[d], pieces, preferred_element_type=jnp.float32)
        value = (trial[d] - slope).astype(jnp.bfloat16)
        vel[d] = value
        for k in range(8):
            wide[64 * d : 64 * d + 64, LANES * k : LANES * (k + 1)] = value[64 * k : 64 * k + 64]
        speed = speed + jnp.abs(value.astype(jnp.float32))
    open_sums(0, 0, jnp.max(speed, axis=0, keepdims=True))

    element = lax.broadcasted_iota(jnp.int32, (LANES, LANES), 0).astype(jnp.float32)
    own_first = (me[0] * LANES).astype(jnp.float32)

    def interpolate(source, target, first, end):
        def lagrange(point):
            value = table_ref[7]
            for j in range(7):
                value = value * (point - table_ref[j])
            return value

        def spread(row):
            row = jnp.broadcast_to(row, (16, LANES)).astype(jnp.bfloat16)
            return jnp.concatenate([row] * (LANES // 16), axis=0)

        def one_tile(i, carry):
            chosen = []
            weights = []
            for h in range(2):
                row = pl.ds(2 * i + h, 1)
                key = source[3, row, :] - own_first
                hot = jnp.where(element == key, 1.0, 0.0).astype(jnp.bfloat16)
                w_x, w_y, w_z = (lagrange(source[axis, row, :]) for axis in range(3))
                weights.append((w_y, w_z))
                chosen.append(
                    jnp.concatenate([hot * spread(w_x[k : k + 1]) for k in range(8)], axis=0)
                )
            taken = jnp.dot(
                wide[...],
                jnp.concatenate(chosen, axis=1),
                preferred_element_type=jnp.float32,
            )
            for d in range(3):
                for h in range(2):
                    part = taken[64 * d : 64 * d + 64, h * LANES : (h + 1) * LANES]
                    w_y, w_z = weights[h]
                    over_y = w_y[0:1] * part[0:8]
                    for l in range(1, 8):
                        over_y = over_y + w_y[l : l + 1] * part[8 * l : 8 * l + 8]
                    target[d, pl.ds(2 * i + h, 1), :] = jnp.sum(
                        w_z * over_y, axis=0, keepdims=True
                    )
            return carry

        lax.fori_loop(first, end, one_tile, 0, unroll=UNROLL)

    def finish_faces():
        drain_faces(last - 1)
        close_faces(last, (img,))
        left = res[...] - img[...]
        open_sums(1, 0, jnp.sum(left * left, axis=0, keepdims=True))

    tiles = groups // 2
    half = tiles // 2
    turn = 0
    for offset in order:
        pay_copy(offset).wait_recv()
        for first, end in ((0, half), (half, tiles)):
            interpolate(pay_in.at[offset - 1], back_out.at[offset], first, end)
            if end == tiles:
                back_copy(offset).start()
            turn += 1
            if turn == FINISH:
                finish_faces()
    if turn < FINISH:
        finish_faces()
    interpolate(pay_ref, back_out.at[0], 0, tiles)

    drain_faces(last)
    most = close_sums(0, 0)
    for t in range(1, len(teams)):
        open_sums(0, t, most)
        open_sums(1, t, close_sums(1, t - 1))
        most = close_sums(0, t)
    stride = courant / (jnp.max(most, axis=1, keepdims=True) + 1e-06)
    stride = jnp.broadcast_to(stride, (groups, LANES))
    drain_sums(0)
    settle(back_in, back_send.at[0])
    settle(back_in, back_recv.at[0])
    for d in range(3):
        flow = back_out[0, d]
        for offset in range(1, line):
            flow = flow + back_in[offset - 1, d]
        moved = pay_ref[d] + stride * (1.5 * flow - 0.5 * old_ref[d])
        for g in range(groups):
            flow_ref[d : d + 1, g * LANES : (g + 1) * LANES] = flow[g : g + 1]
            moved_ref[d : d + 1, g * LANES : (g + 1) * LANES] = moved[g : g + 1]

    drain_sums(1)
    total = jnp.sum(close_sums(1, len(teams) - 1), axis=1, keepdims=True)
    power_ref[...] = jnp.broadcast_to(
        total * (1.0 / (float(NODES * LANES) * sizes[0] * sizes[1] * sizes[2])), (8, LANES)
    )


def write_out(*refs):
    count = (len(refs) - 2) // 2
    sources, targets = refs[:count], refs[count : 2 * count]
    held, given = refs[2 * count :]
    outward = [pltpu.make_async_copy(sources[i], targets[i], given.at[i]) for i in range(1, count)]
    outward.append(pltpu.make_async_copy(held, targets[0], given.at[0]))
    for copy in outward[:-1]:
        copy.start()
    held[0, 0] = sources[0][0, 0]
    outward[-1].start()
    for copy in outward:
        copy.wait()


def per_device(
    sizes,
    element_ops,
    load_terms,
    trial_velocity,
    tracer_coords,
    tracer_old_velocity,
    host_line,
    host_element_index,
):
    count = host_element_index.shape[0]
    groups = count // LANES
    line = sizes[0]
    direct = max(sizes) <= SWEEPS
    seats = sizes[0] * sizes[1] * sizes[2] if direct else sizes[0] + sizes[1] * sizes[2]
    matrix = jnp.asarray(gradient_matrix()).reshape(3, FINE, 4 * NODES)
    f32 = jnp.float32
    i32 = jnp.int32
    bf16 = jnp.bfloat16
    hbm = pl.BlockSpec(memory_space=pltpu.HBM)
    vmem = pl.BlockSpec(memory_space=pltpu.VMEM)
    dma = pltpu.SemaphoreType.DMA
    small = [pltpu.VMEM((NODES, LANES), f32)] * 4
    operands = (
        element_ops,
        load_terms,
        trial_velocity,
        matrix,
        jnp.asarray(weight_table()),
        tracer_coords,
        tracer_old_velocity,
        host_line.reshape(groups, LANES),
        host_element_index.reshape(groups, LANES),
    )
    solution, velocity, power, flows, moved = pl.pallas_call(
        functools.partial(kernel, sizes, direct),
        out_shape=(
            pltpu.VMEM((NODES, LANES), f32),
            pltpu.VMEM((3, FINE, LANES), bf16),
            pltpu.VMEM((8, LANES), f32),
            pltpu.VMEM((3, count), f32),
            pltpu.VMEM((3, count), f32),
        ),
        in_specs=[hbm] * 9,
        out_specs=(vmem,) * 5,
        scratch_shapes=[
            pltpu.VMEM((NODES, NODES, LANES), f32),
            pltpu.VMEM((NODES, LANES), f32),
            pltpu.VMEM((3, FINE, LANES), f32),
            pltpu.VMEM((3, FINE, 4 * NODES), bf16),
            pltpu.VMEM((8, 8, LANES), f32),
            pltpu.VMEM((3, count), f32),
            pltpu.VMEM((3, count), f32),
            pltpu.VMEM((groups, LANES), i32),
            pltpu.VMEM((groups, LANES), i32),
            pltpu.VMEM((4, groups, LANES), f32),
            pltpu.VMEM((3, groups, LANES), f32),
            *small,
            pltpu.VMEM((4, 40, LANES), f32),
            pltpu.VMEM((3 * NODES, 8 * LANES), bf16),
            pltpu.VMEM((NODES // 8, 8, 8, LANES), f32),
            pltpu.VMEM((20 * FACE, LANES), f32),
            pltpu.VMEM((SWEEPS + 1, 27, 2 * FACE, LANES), f32),
            pltpu.VMEM((SWEEPS + 1, 27, 2 * FACE, LANES), f32),
            pltpu.VMEM((line - 1, 4, groups, LANES), f32),
            pltpu.VMEM((line, 3, groups, LANES), f32),
            pltpu.VMEM((line - 1, 3, groups, LANES), f32),
            pltpu.VMEM((2, 2, 8, LANES), f32),
            pltpu.VMEM((2, seats, 8, LANES), f32),
            dma((10,)),
            dma((2,)),
            dma((2,)),
            dma((1,)),
            dma((line - 1,)),
            dma((1,)),
            dma((1,)),
            dma((2, 1 if direct else 2)),
            dma((2, 1 if direct else 2)),
        ],
        compiler_params=pltpu.CompilerParams(
            collective_id=0, has_side_effects=True, vmem_limit_bytes=BRICK_VMEM
        ),
        name="brick",
    )(*(pltpu.with_memory_space_constraint(operand, pltpu.HBM) for operand in operands))
    results = (power, solution, velocity, flows, moved)
    shapes = ((1, 1),) + tuple(r.shape for r in results[1:])
    power, solution, velocity, flows, moved = pl.pallas_call(
        write_out,
        out_shape=tuple(jax.ShapeDtypeStruct(z, r.dtype) for z, r in zip(shapes, results)),
        in_specs=[vmem] + [pl.BlockSpec(memory_space=pl.ANY)] * 4,
        out_specs=(hbm,) * 5,
        scratch_shapes=[pltpu.SMEM((1, 1), f32), dma((5,))],
        compiler_params=pltpu.CompilerParams(vmem_limit_bytes=OUT_VMEM),
        name="write_out",
    )(*results)
    return (solution, velocity, power.reshape(()), flows, moved)


def solution(mesh):
    sizes = tuple(mesh.shape[axis] for axis in AXES)
    placed = (
        P(None, None, AXES),
        P(None, AXES),
        P(None, None, AXES),
        P(None, AXES),
        P(None, AXES),
        P(AXES, None),
        P(AXES),
    )
    return jax.shard_map(
        functools.partial(per_device, sizes),
        mesh=mesh,
        in_specs=placed,
        out_specs=(
            P(None, AXES),
            P(None, None, AXES),
            P(),
            P(None, AXES),
            P(None, AXES),
        ),
        check_vma=False,
    )
```
